1024 devices in a mesh: member: 16 (over y, core), dx: 16 (over x, z_hi), dy: 4 (over z_lo).
Axes of the slice: x: 8, y: 8, z: 8 (z_hi: 2, z_lo: 4; z = z_hi * 4 + z_lo), core: 2. Of those that a mesh axis runs over, the one named last changes fastest.
Arguments:
- perturbed_states: float32 [16, 4, 8, 256, 512], P('member', None, None, 'dx', 'dy'), may hold values from -6 to 6
- control: float32 [16, 4, 8, 256, 512], P('member', None, None, 'dx', 'dy'), may hold values from -6 to 6
- owner: int32 [16], replicated, may hold values from 0 to 15, each once
- map_factor: float32 [256, 512], P('dx', 'dy'), may hold values from 0.5 to 2
- terrain: int32 [256, 512], P('dx', 'dy'), may hold values from 0 to 3
Outputs:
- forecast: float32 [16, 4, 8, 256, 512], P('member', None, None, 'dx', 'dy')
The draws below stay inside these ranges and needn't reach their ends.
Inputs may be any that keep to these rules, and one draw needn't show every extreme that they name: `owner`: a permutation of the member indices.
All inputs are finite; a program needn't handle non-finite values.
Results may differ from the reference program's by a relative error of at most 0.0003.
Values sent between devices are 32-bit elements; how exact they have to be, the bound alone decides.
A program may use at most 32 MiB of HBM per device.

```python
import math
import jax
import jax.numpy as jnp
from jax import lax

PROGNOSTIC_VARS = 4
LEV = 8
STEPS = 4
ENS = 16
NX = 256
NY = 512


def touch_ends(drawn, own_key, low, top_value):
    spot = [jax.random.randint(jax.random.fold_in(own_key, axis), (), 0, length) for axis, length in enumerate(drawn.shape)]
    longest = drawn.shape.index(max(drawn.shape))
    beside = spot[:longest] + [(spot[longest] + 1) % drawn.shape[longest]] + spot[longest + 1:]
    return drawn.at[tuple(spot)].set(low).at[tuple(beside)].set(top_value)


def steps_of(rng, dims, shards, least, top_value):
    def one(dim, blocks):
        steps = jax.random.uniform(jax.random.fold_in(jax.random.fold_in(rng, 6), dim), (blocks,), jnp.float32, least / len(shards), top_value / len(shards))
        return jnp.repeat(jnp.exp(steps), dims[dim] // blocks).reshape((-1,) + (1,) * (len(dims) - dim - 1))

    gain = one(*shards[0])
    for cut in shards[1:]:
        gain = gain * one(*cut)
    return gain


def scatter_about(rng, shape, scale, most, shards=(), held_as=jnp.bfloat16):
    array = scale * jax.random.normal(rng, shape, jnp.float32)
    if shards:
        array = array * steps_of(rng, shape, shards, -0.22, 0.18)
    return jnp.clip(array, -most, most).astype(held_as)


def setup_inputs(seed: int = 0) -> dict:
    seeds = jax.random.split(jax.random.key(seed), 6)
    perturbed_states = scatter_about(seeds[0], (ENS, PROGNOSTIC_VARS, LEV, NX, NY), 1.0, 6.0, ((0, 16), (3, 16), (4, 4)), jnp.float32)
    control = scatter_about(seeds[1], (ENS, PROGNOSTIC_VARS, LEV, NX, NY), 1.0, 6.0, ((0, 16), (3, 16), (4, 4)), jnp.float32)
    owner = jax.random.permutation(seeds[2], ENS).astype(jnp.int32)
    map_factor = jnp.clip(jnp.exp(math.log(2.0) - 1.3862944 * jax.random.uniform(seeds[3], (NX, NY), jnp.float32) ** steps_of(seeds[3], (NX, NY), ((0, 16), (1, 4)), -0.2, 0.2)), 0.5, 2.0)
    terrain = touch_ends(jax.random.randint(seeds[4], (NX, NY), 0, LEV // 2), jax.random.fold_in(seeds[4], 1), 0, (LEV // 2) - 1).astype(jnp.int32)
    return dict(perturbed_states=perturbed_states, control=control, owner=owner, map_factor=map_factor, terrain=terrain)


integration_step = 0.2
diffusion = 0.1


def advance(padded, metric, vertical_level_mask):
    middle_point = padded[:, :, 1:-1, 1:-1]
    east = padded[:, :, 2:, 1:-1]
    west = padded[:, :, :-2, 1:-1]
    north = padded[:, :, 1:-1, 2:]
    south = padded[:, :, 1:-1, :-2]
    gradient_along_x = (east - west) * 0.5
    grad_y = (north - south) * 0.5
    stacked = jnp.pad(middle_point, ((0, 0), (1, 1), (0, 0), (0, 0)))
    laplace = east + west + north + south + stacked[:, 2:] + stacked[:, :-2] - 6.0 * middle_point
    wind_x = middle_point[0]
    meridional_velocity = middle_point[1]
    trend = -metric * (wind_x * gradient_along_x + meridional_velocity * grad_y) + diffusion * laplace
    extra = jnp.stack([-metric * gradient_along_x[2], -metric * grad_y[2], -metric * (gradient_along_x[0] + grad_y[1]), jnp.zeros_like(wind_x)])
    return vertical_level_mask * (middle_point + integration_step * (trend + extra))


def rank_weights(owner):
    ranks = lax.broadcasted_iota(jnp.int32, (ENS, ENS), 0)
    members = lax.broadcasted_iota(jnp.int32, (ENS, ENS), 1)
    per_rank = 2.0 * (ENS - ranks.astype(jnp.float32)) / (ENS * (ENS + 1.0))
    hits = owner[:, None].astype(jnp.int32) == members
    return jnp.sum(jnp.where(hits, per_rank, jnp.zeros_like(per_rank)), axis=0)


def reference(perturbed_states, control, owner, map_factor, terrain):
    mean = jnp.sum(perturbed_states, axis=0) / ENS
    weight = rank_weights(owner)
    chosen = jnp.tensordot(weight, control, axes=1)
    levels = lax.broadcasted_iota(jnp.int32, (LEV, NX, NY), 0)
    vertical_level_mask = (levels >= terrain[None].astype(jnp.int32)).astype(jnp.float32)

    def predict_sample_state(sample_state):
        state = chosen + sample_state - mean
        for number in range(STEPS):
            padded = jnp.pad(state, ((0, 0), (0, 0), (1, 1), (1, 1)))
            state = advance(padded, map_factor, vertical_level_mask)
        return state

    return lax.map(predict_sample_state, perturbed_states)
```

```python
import functools

import jax
import jax.numpy as jnp
from jax import lax
from jax.experimental import pallas as pl
from jax.experimental.pallas import tpu as pltpu
from jax.sharding import PartitionSpec as P

MESH = pl.DeviceIdType.MESH
F32 = jnp.float32

STEPS = 4
FIELDS = 4
LEV = 8
ROWS = 16
COLS = 128
WIDTH = STEPS
TALL = ROWS + 2 * WIDTH
GROUPS = 4
STRIP = TALL // GROUPS
METRIC, MASK = FIELDS, FIELDS + 1
TILE = (LEV, COLS)

integration_step = 0.2
diffusion = 0.1


def stencil(src, dst, b, metric, mask, level):
    mid = [src[b, f] for f in range(FIELDS)]
    east = [src[b + 1, f] for f in range(FIELDS)]
    west = [src[b - 1, f] for f in range(FIELDS)]
    along_x = metric * mid[0]
    along_y = metric * mid[1]
    new, gx, gy = [], [], []
    for f in range(FIELDS):
        north = pltpu.roll(mid[f], COLS - 1, 1)
        south = pltpu.roll(mid[f], 1, 1)
        above = jnp.where(level < LEV - 1, pltpu.roll(mid[f], LEV - 1, 0), 0.0)
        below = jnp.where(level > 0, pltpu.roll(mid[f], 1, 0), 0.0)
        gx.append(east[f] - west[f])
        gy.append(north - south)
        six = (east[f] + west[f]) + (north + south) + (above + below)
        flow = along_x * gx[f] + along_y * gy[f]
        rate = integration_step * diffusion
        new.append((1.0 - 6.0 * rate) * mid[f] + rate * six + flow)
    new[0] = new[0] + metric * gx[2]
    new[1] = new[1] + metric * gy[2]
    new[2] = new[2] + metric * (gx[0] + gy[1])
    for f in range(FIELDS):
        dst[b, f] = mask * new[f]


def kernel(
    members, nx, ny,
    p_hbm, c_hbm, owner_hbm, map_hbm, ter_hbm, out_hbm,
    pv, cv, ov, owner, mv, tv, s0, s1, q, qr, t, rr, dx_rows, mts, mtr, a0, a1, es, er,
    local_sem, dd_s, dd_r, rs_s, rs_r, ag_s, ag_r, fw_s, fw_r, hx_s, hx_r, ha_s, ha_r, hf_s, hf_r,
    ph_s, ph_r, mt_s, mt_r, ed_s, ed_r,
):
    chips = members // 2
    part = (ROWS // 2) // chips
    me = lax.axis_index("member")
    x = lax.axis_index("dx")
    y = lax.axis_index("dy")
    chip = lax.div(me, 2)
    core = lax.rem(me, 2)
    partner = {"member": me + 1 - 2 * core}
    has_w, has_e = x > 0, x < nx - 1
    has_s, has_n = y > 0, y < ny - 1

    def peer(d):
        return lax.rem(chip + d, chips)

    def source(d):
        return lax.rem(chip + chips - d, chips)

    def top(ch):
        return lax.div(2 * ch, chips)

    def own_b(co, ch):
        return WIDTH + ch * part + (1 - co) * (ROWS // 2) * top(ch) + co * WIDTH

    def halo_b(ch):
        return ch * part + (WIDTH + ROWS) - TALL * top(ch)

    def came_from(ch):
        at = x + 1 - 2 * top(ch)
        return jnp.logical_and(at >= 0, at < nx)

    def remote(src, dst, ss, rs, device):
        return pltpu.make_async_remote_copy(
            src_ref=src, dst_ref=dst, send_sem=ss, recv_sem=rs, device_id=device, device_id_type=MESH
        )

    loads = [
        pltpu.make_async_copy(p_hbm, pv, local_sem.at[0]),
        pltpu.make_async_copy(c_hbm, cv, local_sem.at[1]),
        pltpu.make_async_copy(owner_hbm, owner, local_sem.at[2]),
        pltpu.make_async_copy(map_hbm, mv, local_sem.at[3]),
        pltpu.make_async_copy(ter_hbm, tv, local_sem.at[4]),
    ]
    for load in loads:
        load.start()
    barrier = pltpu.get_barrier_semaphore()

    def greet(device):
        pl.semaphore_signal(barrier, inc=1, device_id=device, device_id_type=MESH)

    pl.when(has_w)(lambda: greet({"dx": x - 1}))
    pl.when(has_e)(lambda: greet({"dx": x + 1}))
    for d in range(1, chips):
        greet({"member": 2 * peer(d) + core})
    greet(partner)
    pl.when(has_s)(lambda: greet({"dy": y - 1}))
    pl.when(has_n)(lambda: greet({"dy": y + 1}))

    level = lax.broadcasted_iota(jnp.int32, TILE, 0)
    lane = lax.broadcasted_iota(jnp.int32, TILE, 1)
    level_f = level.astype(F32)
    zero = jnp.zeros(TILE, F32)

    for load in loads:
        load.wait()
    weight = F32(0.0)
    for rank in range(members):
        value = 2.0 * (members - rank) / (members * (members + 1.0))
        weight = weight + jnp.where(owner[rank] == me, F32(value), F32(0.0))

    def first(r, carry):
        for f in range(FIELDS):
            state = pv[pl.ds(f * LEV * ROWS + r, LEV, stride=ROWS), :]
            other = cv[pl.ds(f * LEV * ROWS + r, LEV, stride=ROWS), :]
            s0[r + WIDTH, f] = state
            q[r, f] = weight * other - (1.0 / members) * state
        return carry

    lax.fori_loop(0, ROWS, first, 0, unroll=2)
    for side, start in ((0, 0), (1, ROWS - WIDTH)):
        mts[side, pl.ds(0, WIDTH), :] = mv[pl.ds(start, WIDTH), :]
        mts[side, pl.ds(WIDTH, WIDTH), :] = tv[pl.ds(start, WIDTH), :].astype(F32)

    def empty(b0, side):
        def body():
            for b in range(WIDTH):
                for f in range(FIELDS):
                    s0[b0 + b, f] = zero
                    dx_rows[b0 + b, f] = zero
            mtr[side, pl.ds(0, WIDTH), :] = jnp.ones((WIDTH, COLS), F32)
            mtr[side, pl.ds(WIDTH, WIDTH), :] = jnp.full((WIDTH, COLS), F32(2 * LEV))
        return body

    pl.when(jnp.logical_not(has_w))(empty(0, 1))
    pl.when(jnp.logical_not(has_e))(empty(WIDTH + ROWS, 0))

    def no_edge(side):
        def body():
            for f in range(FIELDS + 2):
                er[side, f] = zero
        return body

    pl.when(jnp.logical_not(has_s))(no_edge(0))
    pl.when(jnp.logical_not(has_n))(no_edge(1))

    pl.semaphore_wait(
        barrier,
        chips + has_w.astype(jnp.int32) + has_e.astype(jnp.int32) + has_s.astype(jnp.int32) + has_n.astype(jnp.int32),
    )

    far_first = sorted(range(1, chips), key=lambda d: -min(d, chips - d))
    near_first = far_first[::-1]
    order = far_first + [0]

    def dd(i):
        ch = peer(order[i])
        return remote(
            q.at[pl.ds(own_b(1 - core, ch) - WIDTH, part)], qr.at[pl.ds(ch * part, part)],
            dd_s.at[i], dd_r.at[i], partner,
        )

    for i in range(chips):
        dd(i).start()

    def p_halo(side):
        src, dst, step = ((WIDTH, WIDTH + ROWS, -1), (ROWS, 0, 1))[side]
        return remote(
            s0.at[pl.ds(src, WIDTH), pl.ds(0, FIELDS)], s0.at[pl.ds(dst, WIDTH), pl.ds(0, FIELDS)],
            ph_s.at[side], ph_r.at[side], {"dx": x + step},
        )

    def mt_halo(side):
        return remote(mts.at[side], mtr.at[side], mt_s.at[side], mt_r.at[side], {"dx": x + (-1, 1)[side]})

    def to_west():
        mt_halo(0).start()
        p_halo(0).start()

    def to_east():
        mt_halo(1).start()
        p_halo(1).start()

    pl.when(has_w)(to_west)
    pl.when(has_e)(to_east)

    def rs(d):
        return remote(
            t.at[pl.ds(peer(d) * part, part)], rr.at[pl.ds((d - 1) * part, part)],
            rs_s.at[d - 1], rs_r.at[d - 1], {"member": 2 * peer(d) + core},
        )

    for i, d in enumerate(order):
        dd(i).wait_recv()
        ch = peer(d)
        for n in range(part):
            for f in range(FIELDS):
                t[ch * part + n, f] = q[own_b(core, ch) - WIDTH + n, f] + qr[ch * part + n, f]
        if d:
            rs(d).start()

    def factors(r, carry):
        s0[r + WIDTH, METRIC] = jnp.broadcast_to(mv[pl.ds(r, 1), :] * (-0.5 * integration_step), TILE)
        ground = jnp.broadcast_to(tv[pl.ds(r, 1), :], TILE)
        s0[r + WIDTH, MASK] = (level >= ground).astype(F32)
        return carry

    lax.fori_loop(0, ROWS, factors, 0)

    total = [[t[chip * part + n, f] for f in range(FIELDS)] for n in range(part)]
    for d in near_first:
        rs(d).wait_recv()
        for n in range(part):
            for f in range(FIELDS):
                total[n][f] = total[n][f] + rr[(d - 1) * part + n, f]
    mine = own_b(core, chip)
    for n in range(part):
        for f in range(FIELDS):
            dx_rows[mine + n, f] = total[n][f]

    here = pl.ds(mine, part)
    halo_here = pl.ds(halo_b(chip), part)
    lead = core == 0
    at = x + 2 * top(chip) - 1
    gives = jnp.logical_and(lead, jnp.logical_and(at >= 0, at < nx))
    takes = jnp.logical_and(lead, came_from(chip))
    hx = remote(dx_rows.at[here], dx_rows.at[halo_here], hx_s, hx_r, {"dx": at})
    pl.when(gives)(hx.start)

    def ag(d):
        return remote(
            dx_rows.at[here], dx_rows.at[here], ag_s.at[d - 1], ag_r.at[d - 1], {"member": 2 * peer(d) + core}
        )

    def ha(d):
        return remote(
            dx_rows.at[halo_here], dx_rows.at[halo_here], ha_s.at[d - 1], ha_r.at[d - 1],
            {"member": 2 * peer(d) + core},
        )

    def fw(d):
        rows = pl.ds(own_b(core, source(d)), part)
        return remote(dx_rows.at[rows], dx_rows.at[rows], fw_s.at[d], fw_r.at[d], partner)

    def hf(d):
        rows = pl.ds(halo_b(source(d)), part)
        return remote(dx_rows.at[rows], dx_rows.at[rows], hf_s.at[d], hf_r.at[d], partner)

    for d in far_first:
        ag(d).start()
    fw(0).start()

    def halo_factors(side, b0):
        for b in range(WIDTH):
            s0[b0 + b, METRIC] = jnp.broadcast_to(mtr[side, pl.ds(b, 1), :] * (-0.5 * integration_step), TILE)
            ground = jnp.broadcast_to(mtr[side, pl.ds(WIDTH + b, 1), :], TILE)
            s0[b0 + b, MASK] = (level_f >= ground).astype(F32)

    pl.when(has_e)(lambda: mt_halo(0).wait_recv())
    pl.when(has_w)(lambda: mt_halo(1).wait_recv())
    halo_factors(0, WIDTH + ROWS)
    halo_factors(1, 0)

    inner = lax.rem(lane, 16)
    block = lax.div(lane, 16)

    def strip_fields(fields):
        def body(i, carry):
            for f in fields:
                packed = zero
                for g in range(GROUPS):
                    row = s0[g * STRIP + i, f]
                    left = jnp.logical_and(block == g, inner >= WIDTH)
                    right = jnp.logical_and(block == GROUPS + g, inner < 16 - WIDTH)
                    packed = jnp.where(left, pltpu.roll(row, 16 * g + WIDTH, 1), packed)
                    packed = jnp.where(right, pltpu.roll(row, 16 * g + 76, 1), packed)
                a0[i + 1, f] = packed
            return carry

        lax.fori_loop(0, STRIP, body, 0)

    strip_fields((METRIC, MASK))

    for d in near_first:
        ag(d).wait_recv()
        fw(d).start()

    def spread_halo():
        hx.wait_recv()
        for d in far_first:
            ha(d).start()
        hf(0).start()

    pl.when(takes)(spread_halo)
    for d in near_first:
        def pass_on(d=d):
            ha(d).wait_recv()
            hf(d).start()

        pl.when(jnp.logical_and(lead, came_from(source(d))))(pass_on)

    for d in [0] + near_first:
        fw(d).wait_recv()
    pl.when(has_w)(lambda: p_halo(0).wait_send())
    pl.when(has_e)(lambda: p_halo(1).wait_send())
    pl.when(has_e)(lambda: p_halo(0).wait_recv())
    pl.when(has_w)(lambda: p_halo(1).wait_recv())
    for d in [0] + near_first:
        pl.when(jnp.logical_and(core == 1, came_from(source(d))))(lambda d=d: hf(d).wait_recv())

    def begin(b, carry):
        for f in range(FIELDS):
            s0[b, f] = s0[b, f] + dx_rows[b, f]
        return carry

    lax.fori_loop(0, TALL, begin, 0, unroll=2)

    strip_fields(range(FIELDS))
    for f in range(FIELDS + 2):
        north, south = zero, zero
        for i in range(STRIP):
            strip = a0[i + 1, f]
            at_lane = (i // 4) * 64 + (i % 4) * 4
            slot = jnp.logical_and(lax.div(lane, 64) == i // 4, lax.div(inner, 4) == i % 4)
            north = jnp.where(slot, pltpu.roll(strip, (at_lane - 72) % COLS, 1), north)
            south = jnp.where(slot, pltpu.roll(strip, (at_lane - 4) % COLS, 1), south)
        es[0, f] = north
        es[1, f] = south

    def edge(side):
        return remote(es.at[side], er.at[side], ed_s.at[side], ed_r.at[side], {"dy": y + (1, -1)[side]})

    pl.when(has_n)(lambda: edge(0).start())
    pl.when(has_s)(lambda: edge(1).start())

    for step in range(STEPS):
        src, dst = (s0, s1) if step % 2 == 0 else (s1, s0)

        def row(b, carry, src=src, dst=dst):
            stencil(src, dst, b, s0[b, METRIC], s0[b, MASK], level)
            return carry

        lax.fori_loop(step + 1, TALL - step - 1, row, 0, unroll=2)

    pl.when(has_s)(lambda: edge(0).wait_recv())
    pl.when(has_n)(lambda: edge(1).wait_recv())
    for i in range(STRIP):
        at_lane = (i // 4) * 64 + (i % 4) * 4
        left = jnp.logical_and(block < GROUPS, inner < WIDTH)
        right = jnp.logical_and(block >= GROUPS, inner >= 16 - WIDTH)
        for f in range(FIELDS + 2):
            strip = a0[i + 1, f]
            strip = jnp.where(left, pltpu.roll(er[0, f], (-at_lane) % COLS, 1), strip)
            strip = jnp.where(right, pltpu.roll(er[1, f], (76 - at_lane) % COLS, 1), strip)
            a0[i + 1, f] = strip
    for step in range(STEPS):
        src, dst = (a0, a1) if step % 2 == 0 else (a1, a0)
        for f in range(FIELDS):
            src[0, f] = pltpu.roll(src[STRIP, f], 16, 1)
            src[STRIP + 1, f] = pltpu.roll(src[1, f], COLS - 16, 1)

        def strip_row(i, carry, src=src, dst=dst):
            stencil(src, dst, i, a0[i, METRIC], a0[i, MASK], level)
            return carry

        lax.fori_loop(1, STRIP + 1, strip_row, 0, unroll=2)

    for g in range(GROUPS):
        def merge(i, carry, g=g):
            for f in range(FIELDS):
                strip = a0[i + 1, f]
                out = s0[g * STRIP + i, f]
                out = jnp.where(lane < WIDTH, pltpu.roll(strip, (-16 * g - WIDTH) % COLS, 1), out)
                out = jnp.where(lane >= COLS - WIDTH, pltpu.roll(strip, (52 - 16 * g) % COLS, 1), out)
                ov[pl.ds(f * LEV * ROWS + g * STRIP + i - WIDTH, LEV, stride=ROWS), :] = out
            return carry

        lax.fori_loop(max(0, WIDTH - g * STRIP), min(STRIP, WIDTH + ROWS - g * STRIP), merge, 0)
    store = pltpu.make_async_copy(ov, out_hbm, local_sem.at[0])
    store.start()

    for i in range(chips):
        dd(i).wait_send()
    for d in far_first:
        rs(d).wait_send()
        ag(d).wait_send()
    pl.when(gives)(hx.wait_send)

    def halo_sent():
        for d in far_first:
            ha(d).wait_send()

    pl.when(takes)(halo_sent)
    for d in range(chips):
        fw(d).wait_send()
        pl.when(jnp.logical_and(lead, came_from(source(d))))(lambda d=d: hf(d).wait_send())
    pl.when(has_w)(lambda: mt_halo(0).wait_send())
    pl.when(has_e)(lambda: mt_halo(1).wait_send())
    pl.when(has_n)(lambda: edge(0).wait_send())
    pl.when(has_s)(lambda: edge(1).wait_send())
    store.wait()


def solution(mesh):
    members, nx, ny = (mesh.shape[axis] for axis in ("member", "dx", "dy"))
    chips = members // 2
    part = (ROWS // 2) // chips
    flat = FIELDS * LEV * ROWS

    def on_device(states, control, owner, map_factor, terrain):
        any_space = pl.BlockSpec(memory_space=pl.ANY)
        dma = pltpu.SemaphoreType.DMA
        out = pl.pallas_call(
            functools.partial(kernel, members, nx, ny),
            out_shape=jax.ShapeDtypeStruct((flat, COLS), F32),
            in_specs=[any_space] * 5,
            out_specs=any_space,
            scratch_shapes=[
                pltpu.VMEM((flat, COLS), F32),
                pltpu.VMEM((flat, COLS), F32),
                pltpu.VMEM((flat, COLS), F32),
                pltpu.SMEM((members,), jnp.int32),
                pltpu.VMEM((ROWS, COLS), F32),
                pltpu.VMEM((ROWS, COLS), jnp.int32),
                pltpu.VMEM((TALL, FIELDS + 2) + TILE, F32),
                pltpu.VMEM((TALL, FIELDS) + TILE, F32),
                pltpu.VMEM((ROWS, FIELDS) + TILE, F32),
                pltpu.VMEM((ROWS // 2, FIELDS) + TILE, F32),
                pltpu.VMEM((ROWS // 2, FIELDS) + TILE, F32),
                pltpu.VMEM((part * max(chips - 1, 1), FIELDS) + TILE, F32),
                pltpu.VMEM((TALL, FIELDS) + TILE, F32),
                pltpu.VMEM((2,) + TILE, F32),
                pltpu.VMEM((2,) + TILE, F32),
                pltpu.VMEM((STRIP + 2, FIELDS + 2) + TILE, F32),
                pltpu.VMEM((STRIP + 2, FIELDS) + TILE, F32),
                pltpu.VMEM((2, FIELDS + 2) + TILE, F32),
                pltpu.VMEM((2, FIELDS + 2) + TILE, F32),
                dma((5,)),
                dma((chips,)), dma((chips,)),
                dma((chips - 1,)), dma((chips - 1,)),
                dma((chips - 1,)), dma((chips - 1,)),
                dma((chips,)), dma((chips,)),
                dma, dma,
                dma((chips - 1,)), dma((chips - 1,)),
                dma((chips,)), dma((chips,)),
                dma((2,)), dma((2,)),
                dma((2,)), dma((2,)),
                dma((2,)), dma((2,)),
            ],
            compiler_params=pltpu.CompilerParams(collective_id=0, has_side_effects=True),
        )(states.reshape(flat, COLS), control.reshape(flat, COLS), owner, map_factor, terrain)
        return out.reshape(states.shape)

    spread = P("member", None, None, "dx", "dy")
    return jax.shard_map(
        on_device,
        mesh=mesh,
        in_specs=(spread, spread, P(), P("dx", "dy"), P("dx", "dy")),
        out_specs=spread,
        check_vma=False,
    )
```

```python
import functools

import jax
import jax.numpy as jnp
from jax import lax
from jax.experimental import pallas as pl
from jax.experimental.pallas import tpu as pltpu
from jax.sharding import PartitionSpec as P

MESH = pl.DeviceIdType.MESH
F32 = jnp.float32

STEPS = 4
FIELDS = 4
HALF = FIELDS // 2
LEV = 8
ROWS = 16
COLS = 128
WIDTH = STEPS
TALL = ROWS + 2 * WIDTH
GROUPS = 4
STRIP = TALL // GROUPS
METRIC, MASK = FIELDS, FIELDS + 1
TILE = (LEV, COLS)

integration_step = 0.2
diffusion = 0.1


def stencil(src, dst, b, metric, mask, level):
    mid = [src[b, f] for f in range(FIELDS)]
    east = [src[b + 1, f] for f in range(FIELDS)]
    west = [src[b - 1, f] for f in range(FIELDS)]
    along_x = metric * mid[0]
    along_y = metric * mid[1]
    new, gx, gy = [], [], []
    for f in range(FIELDS):
        north = pltpu.roll(mid[f], COLS - 1, 1)
        south = pltpu.roll(mid[f], 1, 1)
        above = jnp.where(level < LEV - 1, pltpu.roll(mid[f], LEV - 1, 0), 0.0)
        below = jnp.where(level > 0, pltpu.roll(mid[f], 1, 0), 0.0)
        gx.append(east[f] - west[f])
        gy.append(north - south)
        six = (east[f] + west[f]) + (north + south) + (above + below)
        flow = along_x * gx[f] + along_y * gy[f]
        rate = integration_step * diffusion
        new.append((1.0 - 6.0 * rate) * mid[f] + rate * six + flow)
    new[0] = new[0] + metric * gx[2]
    new[1] = new[1] + metric * gy[2]
    new[2] = new[2] + metric * (gx[0] + gy[1])
    for f in range(FIELDS):
        dst[b, f] = mask * new[f]


def kernel(
    members, nx, ny,
    p_hbm, c_hbm, owner_hbm, map_hbm, ter_hbm, out,
    pv, cv, owner, mv, tv, s0, s1, s2, s3, s4, q, qr, t, rr, dx_rows, mts, mtr, a0, a1, es, er, hs, hr,
    local_sem, out_s, dd_r, dm_r, rs_r, ag_r, fw_r, hx_s, hx_r, ha_s, ha_r, hf_s, hf_r,
    ph_s, ph_r, mt_s, mt_r, ed_s, ed_r,
):
    chips = members // 2
    part = (ROWS // 2) // chips
    me = lax.axis_index("member")
    x = lax.axis_index("dx")
    y = lax.axis_index("dy")
    chip = lax.div(me, 2)
    core = lax.rem(me, 2)
    partner = {"member": me + 1 - 2 * core}
    has_w, has_e = x > 0, x < nx - 1
    has_s, has_n = y > 0, y < ny - 1
    far_first = sorted(range(1, chips), key=lambda d: -min(d, chips - d))
    near_first = far_first[::-1]
    order = far_first + [0]
    mine = pl.ds(HALF * core, HALF)
    theirs = pl.ds(HALF * (1 - core), HALF)
    sent = []
    pieces = 2 * chips + 2 * (chips - 1) + 2 * (chips - 1) + 2 * chips

    def peer(d):
        return lax.rem(chip + d, chips)

    def source(d):
        return lax.rem(chip + chips - d, chips)

    def top(ch):
        return lax.div(2 * ch, chips)

    def own_b(kind, ch):
        if kind == 0:
            return WIDTH + ch * part + (ROWS // 2) * top(ch)
        return 2 * WIDTH + ch * part

    def halo_b(ch):
        return ch * part + (WIDTH + ROWS) - TALL * top(ch)

    def came_from(ch):
        at = x + 1 - 2 * top(ch)
        return jnp.logical_and(at >= 0, at < nx)

    def remote(src, dst, ss, rs, device):
        return pltpu.make_async_remote_copy(
            src_ref=src, dst_ref=dst, send_sem=ss, recv_sem=rs, device_id=device, device_id_type=MESH
        )

    def arrived(ref, sem):
        pltpu.make_async_copy(ref, ref, sem).wait()

    def same_core(d):
        return {"member": 2 * peer(d) + core}

    loads = [
        pltpu.make_async_copy(p_hbm, pv, local_sem.at[0]),
        pltpu.make_async_copy(c_hbm, cv, local_sem.at[1]),
        pltpu.make_async_copy(owner_hbm, owner, local_sem.at[2]),
        pltpu.make_async_copy(map_hbm, mv, local_sem.at[3]),
        pltpu.make_async_copy(ter_hbm, tv, local_sem.at[4]),
    ]
    for load in loads:
        load.start()
    barrier = pltpu.get_barrier_semaphore()

    def greet(device):
        pl.semaphore_signal(barrier, inc=1, device_id=device, device_id_type=MESH)

    pl.when(has_w)(lambda: greet({"dx": x - 1}))
    pl.when(has_e)(lambda: greet({"dx": x + 1}))
    for d in far_first:
        greet(same_core(d))
    greet(partner)
    pl.when(has_s)(lambda: greet({"dy": y - 1}))
    pl.when(has_n)(lambda: greet({"dy": y + 1}))

    level = lax.broadcasted_iota(jnp.int32, TILE, 0)
    lane = lax.broadcasted_iota(jnp.int32, TILE, 1)
    level_f = level.astype(F32)
    zero = jnp.zeros(TILE, F32)

    for load in loads:
        load.wait()
    weight = F32(0.0)
    for rank in range(members):
        value = 2.0 * (members - rank) / (members * (members + 1.0))
        weight = weight + jnp.where(owner[rank] == me, F32(value), F32(0.0))

    def first(r, carry):
        for f in range(FIELDS):
            state = pv[pl.ds(f * LEV * ROWS + r, LEV, stride=ROWS), :]
            other = cv[pl.ds(f * LEV * ROWS + r, LEV, stride=ROWS), :]
            s0[r + WIDTH, f] = state
            q[r, f] = weight * other - (1.0 / members) * state
        return carry

    lax.fori_loop(0, WIDTH, first, 0, unroll=2)
    lax.fori_loop(ROWS - WIDTH, ROWS, first, 0, unroll=2)
    pl.semaphore_wait(
        barrier,
        chips + has_w.astype(jnp.int32) + has_e.astype(jnp.int32) + has_s.astype(jnp.int32) + has_n.astype(jnp.int32),
    )

    def dd(kind, d):
        rows = pl.ds(own_b(kind, peer(d)) - WIDTH, part)
        return remote(q.at[rows, theirs], qr.at[rows], out_s, dd_r.at[d] if kind == 0 else dm_r, partner)

    def p_halo(side):
        src, dst, step = ((WIDTH, WIDTH + ROWS, -1), (ROWS, 0, 1))[side]
        return remote(
            s0.at[pl.ds(src, WIDTH), pl.ds(0, FIELDS)], s0.at[pl.ds(dst, WIDTH), pl.ds(0, FIELDS)],
            ph_s.at[side], ph_r.at[side], {"dx": x + step},
        )

    def mt_halo(side):
        return remote(mts.at[side], mtr.at[side], mt_s.at[side], mt_r.at[side], {"dx": x + (-1, 1)[side]})

    def rs(kind, d):
        return remote(
            t.at[pl.ds(own_b(kind, peer(d)) - WIDTH, part)], rr.at[kind, pl.ds((d - 1) * part, part)],
            out_s, rs_r.at[kind], same_core(d),
        )

    def swap_and_send(kind):
        if kind == 1:
            arrived(qr.at[pl.ds(WIDTH, ROWS // 2)], dm_r)
        for d in order:
            if kind == 0:
                dd(kind, d).wait_recv()
            b = own_b(kind, peer(d)) - WIDTH
            for n in range(part):
                for f in range(HALF):
                    t[b + n, f] = q[b + n, HALF * core + f] + qr[b + n, f]
            if d:
                rs(kind, d).start()

    for d in order:
        dd(0, d).start()
    pl.when(has_w)(lambda: p_halo(0).start())
    pl.when(has_e)(lambda: p_halo(1).start())
    lax.fori_loop(WIDTH, ROWS - WIDTH, first, 0, unroll=2)
    for d in order:
        dd(1, d).start()
    swap_and_send(0)
    swap_and_send(1)

    for side, start in ((0, 0), (1, ROWS - WIDTH)):
        mts[side, pl.ds(0, WIDTH), :] = mv[pl.ds(start, WIDTH), :]
        mts[side, pl.ds(WIDTH, WIDTH), :] = tv[pl.ds(start, WIDTH), :].astype(F32)
    for side, there in ((0, has_w), (1, has_e)):
        pl.when(there)(lambda side=side: mt_halo(side).start())
        sent.append(lambda side=side, there=there: pl.when(there)(mt_halo(side).wait_send))

    def factors(r, carry):
        s0[r + WIDTH, METRIC] = jnp.broadcast_to(mv[pl.ds(r, 1), :] * (-0.5 * integration_step), TILE)
        ground = jnp.broadcast_to(tv[pl.ds(r, 1), :], TILE)
        s0[r + WIDTH, MASK] = (level >= ground).astype(F32)
        return carry

    lax.fori_loop(0, ROWS, factors, 0)

    def empty(b0, side):
        def body():
            for b in range(WIDTH):
                for f in range(FIELDS):
                    s0[b0 + b, f] = zero
                    dx_rows[b0 + b, f] = zero
            mtr[side, pl.ds(0, WIDTH), :] = jnp.ones((WIDTH, COLS), F32)
            mtr[side, pl.ds(WIDTH, WIDTH), :] = jnp.full((WIDTH, COLS), F32(2 * LEV))
        return body

    pl.when(jnp.logical_not(has_w))(empty(0, 1))
    pl.when(jnp.logical_not(has_e))(empty(WIDTH + ROWS, 0))

    def no_edge(side):
        def body():
            for f in range(FIELDS + 2):
                er[side, f] = zero
            hr[side] = zero
        return body

    pl.when(jnp.logical_not(has_s))(no_edge(0))
    pl.when(jnp.logical_not(has_n))(no_edge(1))

    at = x + 2 * top(chip) - 1
    gives = jnp.logical_and(at >= 0, at < nx)
    takes = came_from(chip)
    halo_here = pl.ds(halo_b(chip), part)
    hx = remote(
        dx_rows.at[pl.ds(own_b(0, chip), part), mine], dx_rows.at[halo_here, mine], hx_s, hx_r, {"dx": at}
    )

    def ag(kind, d):
        rows = pl.ds(own_b(kind, chip), part)
        return remote(
            dx_rows.at[rows, mine], dx_rows.at[rows, mine], out_s, ag_r.at[d - 1], same_core(d)
        )

    def fw(kind, d):
        rows = pl.ds(own_b(kind, source(d)), part)
        return remote(dx_rows.at[rows, mine], dx_rows.at[rows, mine], out_s, fw_r, partner)

    def ha(d):
        return remote(
            dx_rows.at[halo_here, mine], dx_rows.at[halo_here, mine], ha_s, ha_r.at[d - 1], same_core(d)
        )

    def hf(d):
        rows = pl.ds(halo_b(source(d)), part)
        return remote(dx_rows.at[rows, mine], dx_rows.at[rows, mine], hf_s.at[top(source(d))], hf_r.at[top(source(d))], partner)

    for kind in range(2):
        b = own_b(kind, chip)
        total = [[t[b - WIDTH + n, f] for f in range(HALF)] for n in range(part)]
        arrived(rr.at[kind], rs_r.at[kind])
        for d in near_first:
            for n in range(part):
                for f in range(HALF):
                    total[n][f] = total[n][f] + rr[kind, (d - 1) * part + n, f]
        for n in range(part):
            for f in range(HALF):
                dx_rows[b + n, HALF * core + f] = total[n][f]
        if kind == 0:
            pl.when(gives)(hx.start)
            sent.append(lambda: pl.when(gives)(hx.wait_send))
        for d in far_first:
            ag(kind, d).start()
        fw(kind, 0).start()

    def gather(ds):
        for d in ds:
            arrived(dx_rows.at[pl.ds(0, 2 * part), mine], ag_r.at[d - 1])
            for kind in range(2):
                fw(kind, d).start()

    gather(near_first[: chips // 2])
    def spread_halo():
        hx.wait_recv()
        for d in far_first:
            ha(d).start()
        hf(0).start()

    pl.when(takes)(spread_halo)

    sent.append(lambda: pl.when(takes)(lambda: arrived(rr.at[0], ha_s)))
    gather(near_first[chips // 2 :])
    arrived(dx_rows.at[pl.ds(0, ROWS), mine], fw_r)

    pl.when(has_w)(lambda: p_halo(0).wait_send())
    pl.when(has_e)(lambda: p_halo(1).wait_send())

    def begin(b, carry):
        for f in range(FIELDS):
            s0[b, f] = s0[b, f] + dx_rows[b, f]
        return carry

    lax.fori_loop(WIDTH, WIDTH + ROWS, begin, 0, unroll=2)
    states = (s0, s1, s2, s3, s4)
    for step in range(1, STEPS + 1):
        def row(b, carry, src=states[step - 1], dst=states[step]):
            stencil(src, dst, b, s0[b, METRIC], s0[b, MASK], level)
            return carry

        lax.fori_loop(WIDTH + step, WIDTH + ROWS - step, row, 0, unroll=True)

    inner = lax.rem(lane, 16)
    block = lax.div(lane, 16)

    def pack_rows(rows, old):
        def body(f, carry):
            for i in range(STRIP):
                groups = [g for g in range(GROUPS) if g * STRIP + i in rows]
                if not groups:
                    continue
                packed = a0[i + 1, f] if old else zero
                for g in groups:
                    row = s0[g * STRIP + i, f]
                    left = jnp.logical_and(block == g, inner >= WIDTH)
                    right = jnp.logical_and(block == GROUPS + g, inner < 16 - WIDTH)
                    packed = jnp.where(left, pltpu.roll(row, 16 * g + WIDTH, 1), packed)
                    packed = jnp.where(right, pltpu.roll(row, 16 * g + 76, 1), packed)
                a0[i + 1, f] = packed
            return carry
        return body

    inside = range(WIDTH, WIDTH + ROWS)
    outside = [b for b in range(TALL) if b not in inside]
    lax.fori_loop(0, FIELDS + 2, pack_rows(inside, False), 0)

    def halo_factors(side, b0):
        for b in range(WIDTH):
            s0[b0 + b, METRIC] = jnp.broadcast_to(mtr[side, pl.ds(b, 1), :] * (-0.5 * integration_step), TILE)
            ground = jnp.broadcast_to(mtr[side, pl.ds(WIDTH + b, 1), :], TILE)
            s0[b0 + b, MASK] = (level_f >= ground).astype(F32)

    pl.when(has_e)(lambda: mt_halo(0).wait_recv())
    pl.when(has_w)(lambda: mt_halo(1).wait_recv())
    halo_factors(0, WIDTH + ROWS)
    halo_factors(1, 0)
    lax.fori_loop(FIELDS, FIELDS + 2, pack_rows(outside, True), 0)

    for f in range(FIELDS + 2):
        north, south = zero, zero
        for i in range(STRIP):
            strip = a0[i + 1, f]
            at_lane = (i // 4) * 64 + (i % 4) * 4
            slot = jnp.logical_and(lax.div(lane, 64) == i // 4, lax.div(inner, 4) == i % 4)
            north = jnp.where(slot, pltpu.roll(strip, (at_lane - 72) % COLS, 1), north)
            south = jnp.where(slot, pltpu.roll(strip, (at_lane - 4) % COLS, 1), south)
        es[0, f] = north
        es[1, f] = south

    def edge(side):
        return remote(es.at[side], er.at[side], ed_s.at[side], ed_r.at[side], {"dy": y + (1, -1)[side]})

    for side, there in ((0, has_n), (1, has_s)):
        pl.when(there)(lambda side=side: edge(side).start())
        sent.append(lambda side=side, there=there: pl.when(there)(edge(side).wait_send))

    for d in near_first:
        def pass_on(d=d):
            ha(d).wait_recv()
            hf(d).start()

        pl.when(came_from(source(d)))(pass_on)
    pl.when(has_s)(lambda: edge(0).wait_recv())
    pl.when(has_n)(lambda: edge(1).wait_recv())
    for i in range(STRIP):
        at_lane = (i // 4) * 64 + (i % 4) * 4
        left = jnp.logical_and(block < GROUPS, inner < WIDTH)
        right = jnp.logical_and(block >= GROUPS, inner >= 16 - WIDTH)
        for f in range(FIELDS + 2):
            strip = a0[i + 1, f]
            strip = jnp.where(left, pltpu.roll(er[0, f], (-at_lane) % COLS, 1), strip)
            strip = jnp.where(right, pltpu.roll(er[1, f], (76 - at_lane) % COLS, 1), strip)
            a0[i + 1, f] = strip
    for side, there in ((0, has_e), (1, has_w)):
        rows = dx_rows.at[pl.ds(0, WIDTH), mine]
        pl.when(there)(lambda side=side, rows=rows: arrived(rows, hf_r.at[side]))
        sent.append(lambda side=side, there=there, rows=rows: pl.when(there)(lambda: arrived(rows, hf_s.at[side])))
    pl.when(has_e)(lambda: p_halo(0).wait_recv())
    pl.when(has_w)(lambda: p_halo(1).wait_recv())
    lax.fori_loop(0, WIDTH, begin, 0, unroll=2)
    lax.fori_loop(WIDTH + ROWS, TALL, begin, 0, unroll=2)

    lax.fori_loop(0, FIELDS, pack_rows(outside, True), 0)
    north, south = zero, zero
    for f in range(FIELDS):
        for n, b in enumerate(outside):
            at_lane = f * 32 + n * WIDTH
            slot = lax.div(lane, WIDTH) == at_lane // WIDTH
            row = s0[b, f]
            north = jnp.where(slot, pltpu.roll(row, (at_lane + WIDTH) % COLS, 1), north)
            south = jnp.where(slot, pltpu.roll(row, at_lane, 1), south)
    hs[0] = north
    hs[1] = south

    def corner(side):
        return remote(hs.at[side], hr.at[side], ed_s.at[2 + side], ed_r.at[2 + side], {"dy": y + (1, -1)[side]})

    for side, there in ((0, has_n), (1, has_s)):
        pl.when(there)(lambda side=side: corner(side).start())
        sent.append(lambda side=side, there=there: pl.when(there)(corner(side).wait_send))

    for step in range(1, STEPS + 1):
        def rows(j, carry, src=states[step - 1], dst=states[step], step=step):
            for b in (step + j, WIDTH + ROWS - step + j):
                stencil(src, dst, b, s0[b, METRIC], s0[b, MASK], level)
            return carry

        lax.fori_loop(0, WIDTH, rows, 0, unroll=True)

    pl.when(has_s)(lambda: corner(0).wait_recv())
    pl.when(has_n)(lambda: corner(1).wait_recv())
    from_south, from_north = hr[0], hr[1]
    for n, b in enumerate(outside):
        g, i = divmod(b, STRIP)
        left = jnp.logical_and(block == g, inner < WIDTH)
        right = jnp.logical_and(block == GROUPS + g, inner >= 16 - WIDTH)
        for f in range(FIELDS):
            at_lane = f * 32 + n * WIDTH
            strip = a0[i + 1, f]
            strip = jnp.where(left, pltpu.roll(from_south, (16 * g - at_lane) % COLS, 1), strip)
            strip = jnp.where(right, pltpu.roll(from_north, (76 + 16 * g - at_lane) % COLS, 1), strip)
            a0[i + 1, f] = strip
    for step in range(STEPS):
        src, dst = (a0, a1) if step % 2 == 0 else (a1, a0)
        for f in range(FIELDS):
            src[0, f] = pltpu.roll(src[STRIP, f], 16, 1)
            src[STRIP + 1, f] = pltpu.roll(src[1, f], COLS - 16, 1)

        def strip_row(i, carry, src=src, dst=dst):
            stencil(src, dst, i, a0[i, METRIC], a0[i, MASK], level)
            return carry

        lax.fori_loop(1, STRIP + 1, strip_row, 0, unroll=True)

    for g in range(GROUPS):
        def merge(i, carry, g=g):
            for f in range(FIELDS):
                strip = a0[i + 1, f]
                new = s4[g * STRIP + i, f]
                new = jnp.where(lane < WIDTH, pltpu.roll(strip, (-16 * g - WIDTH) % COLS, 1), new)
                new = jnp.where(lane >= COLS - WIDTH, pltpu.roll(strip, (52 - 16 * g) % COLS, 1), new)
                out[pl.ds(f * LEV * ROWS + g * STRIP + i - WIDTH, LEV, stride=ROWS), :] = new
            return carry

        lax.fori_loop(max(0, WIDTH - g * STRIP), min(STRIP, WIDTH + ROWS - g * STRIP), merge, 0, unroll=True)
    arrived(s0.at[pl.ds(0, pieces * part * HALF // (FIELDS + 2))], out_s)
    for wait in sent:
        wait()


def solution(mesh):
    members, nx, ny = (mesh.shape[axis] for axis in ("member", "dx", "dy"))
    chips = members // 2
    part = (ROWS // 2) // chips
    flat = FIELDS * LEV * ROWS

    def on_device(states, control, owner, map_factor, terrain):
        any_space = pl.BlockSpec(memory_space=pl.ANY)
        dma = pltpu.SemaphoreType.DMA
        out = pl.pallas_call(
            functools.partial(kernel, members, nx, ny),
            out_shape=pltpu.VMEM((flat, COLS), F32),
            in_specs=[any_space] * 5,
            out_specs=pl.BlockSpec(memory_space=pltpu.VMEM),
            scratch_shapes=[
                pltpu.VMEM((flat, COLS), F32),
                pltpu.VMEM((flat, COLS), F32),
                pltpu.SMEM((members,), jnp.int32),
                pltpu.VMEM((ROWS, COLS), F32),
                pltpu.VMEM((ROWS, COLS), jnp.int32),
                pltpu.VMEM((TALL, FIELDS + 2) + TILE, F32),
                pltpu.VMEM((TALL, FIELDS) + TILE, F32),
                pltpu.VMEM((TALL, FIELDS) + TILE, F32),
                pltpu.VMEM((TALL, FIELDS) + TILE, F32),
                pltpu.VMEM((TALL, FIELDS) + TILE, F32),
                pltpu.VMEM((ROWS, FIELDS) + TILE, F32),
                pltpu.VMEM((ROWS, HALF) + TILE, F32),
                pltpu.VMEM((ROWS, HALF) + TILE, F32),
                pltpu.VMEM((2, part * (chips - 1), HALF) + TILE, F32),
                pltpu.VMEM((TALL, FIELDS) + TILE, F32),
                pltpu.VMEM((2,) + TILE, F32),
                pltpu.VMEM((2,) + TILE, F32),
                pltpu.VMEM((STRIP + 2, FIELDS + 2) + TILE, F32),
                pltpu.VMEM((STRIP + 2, FIELDS) + TILE, F32),
                pltpu.VMEM((2, FIELDS + 2) + TILE, F32),
                pltpu.VMEM((2, FIELDS + 2) + TILE, F32),
                pltpu.VMEM((2,) + TILE, F32),
                pltpu.VMEM((2,) + TILE, F32),
                dma((5,)),
                dma, dma((chips,)), dma, dma((2,)), dma((chips - 1,)), dma,
                dma, dma,
                dma, dma((chips - 1,)),
                dma((2,)), dma((2,)),
                dma((2,)), dma((2,)),
                dma((2,)), dma((2,)),
                dma((4,)), dma((4,)),
            ],
            compiler_params=pltpu.CompilerParams(collective_id=0, has_side_effects=True),
        )(states.reshape(flat, COLS), control.reshape(flat, COLS), owner, map_factor, terrain)
        return out.reshape(states.shape)

    spread = P("member", None, None, "dx", "dy")
    return jax.shard_map(
        on_device,
        mesh=mesh,
        in_specs=(spread, spread, P(), P("dx", "dy"), P("dx", "dy")),
        out_specs=spread,
        check_vma=False,
    )
```

```python
import functools

import jax
import jax.numpy as jnp
from jax import lax
from jax.experimental import pallas as pl
from jax.experimental.pallas import tpu as pltpu
from jax.sharding import PartitionSpec as P

MESH = pl.DeviceIdType.MESH
F32 = jnp.float32

STEPS = 4
FIELDS = 4
HALF = FIELDS // 2
LEV = 8
ROWS = 16
COLS = 128
WIDTH = STEPS
TALL = ROWS + 2 * WIDTH
GROUPS = 4
STRIP = TALL // GROUPS
METRIC, MASK = FIELDS, FIELDS + 1
TILE = (LEV, COLS)

integration_step = 0.2
diffusion = 0.1


def stencil(src, dst, b, metric, mask, level):
    mid = [src[b, f] for f in range(FIELDS)]
    east = [src[b + 1, f] for f in range(FIELDS)]
    west = [src[b - 1, f] for f in range(FIELDS)]
    along_x = metric * mid[0]
    along_y = metric * mid[1]
    new, gx, gy = [], [], []
    for f in range(FIELDS):
        north = pltpu.roll(mid[f], COLS - 1, 1)
        south = pltpu.roll(mid[f], 1, 1)
        above = jnp.where(level < LEV - 1, pltpu.roll(mid[f], LEV - 1, 0), 0.0)
        below = jnp.where(level > 0, pltpu.roll(mid[f], 1, 0), 0.0)
        gx.append(east[f] - west[f])
        gy.append(north - south)
        six = (east[f] + west[f]) + (north + south) + (above + below)
        flow = along_x * gx[f] + along_y * gy[f]
        rate = integration_step * diffusion
        new.append((1.0 - 6.0 * rate) * mid[f] + rate * six + flow)
    new[0] = new[0] + metric * gx[2]
    new[1] = new[1] + metric * gy[2]
    new[2] = new[2] + metric * (gx[0] + gy[1])
    for f in range(FIELDS):
        dst[b, f] = mask * new[f]


def kernel(
    members, nx, ny,
    p_hbm, c_hbm, owner_hbm, map_hbm, ter_hbm, out,
    pv, cv, owner, mv, tv, s0, s1, s2, s3, s4, q, qr, t, rr, dx_rows, mts, mtr, a0, a1, es, er, pcs, pcr, dcs, crr, crm, cs,
    local_sem, out_s, dd_r, dm_r, rs_r, ag_r, fw_r, hx_s, hx_r, ha_s, ha_r, hf_s, hf_r,
    ph_s, ph_r, mt_s, mt_r, ed_s, ed_r, pc_s, pc_r, dc_s, dc_r, cs_s, cs_r,
):
    chips = members // 2
    part = (ROWS // 2) // chips
    me = lax.axis_index("member")
    x = lax.axis_index("dx")
    y = lax.axis_index("dy")
    chip = lax.div(me, 2)
    core = lax.rem(me, 2)
    partner = {"member": me + 1 - 2 * core}
    has_w, has_e = x > 0, x < nx - 1
    has_s, has_n = y > 0, y < ny - 1
    far_first = sorted(range(1, chips), key=lambda d: -min(d, chips - d))
    near_first = far_first[::-1]
    order = far_first + [0]
    mine = pl.ds(HALF * core, HALF)
    theirs = pl.ds(HALF * (1 - core), HALF)
    sent = []
    pieces = 2 * chips + 2 * (chips - 1) + 2 * (chips - 1) + 2 * chips

    def peer(d):
        return lax.rem(chip + d, chips)

    def source(d):
        return lax.rem(chip + chips - d, chips)

    def top(ch):
        return lax.div(2 * ch, chips)

    def own_b(kind, ch):
        if kind == 0:
            return WIDTH + ch * part + (ROWS // 2) * top(ch)
        return 2 * WIDTH + ch * part

    def halo_b(ch):
        return ch * part + (WIDTH + ROWS) - TALL * top(ch)

    def came_from(ch):
        at = x + 1 - 2 * top(ch)
        return jnp.logical_and(at >= 0, at < nx)

    def remote(src, dst, ss, rs, device):
        return pltpu.make_async_remote_copy(
            src_ref=src, dst_ref=dst, send_sem=ss, recv_sem=rs, device_id=device, device_id_type=MESH
        )

    def arrived(ref, sem):
        pltpu.make_async_copy(ref, ref, sem).wait()

    def same_core(d):
        return {"member": 2 * peer(d) + core}

    loads = [
        pltpu.make_async_copy(p_hbm, pv, local_sem.at[0]),
        pltpu.make_async_copy(c_hbm, cv, local_sem.at[1]),
        pltpu.make_async_copy(owner_hbm, owner, local_sem.at[2]),
        pltpu.make_async_copy(map_hbm, mv, local_sem.at[3]),
        pltpu.make_async_copy(ter_hbm, tv, local_sem.at[4]),
    ]
    for load in loads:
        load.start()
    barrier = pltpu.get_barrier_semaphore()

    def greet(device):
        pl.semaphore_signal(barrier, inc=1, device_id=device, device_id_type=MESH)

    pl.when(has_w)(lambda: greet({"dx": x - 1}))
    pl.when(has_e)(lambda: greet({"dx": x + 1}))
    for d in far_first:
        greet(same_core(d))
    greet(partner)
    pl.when(has_s)(lambda: greet({"dy": y - 1}))
    pl.when(has_n)(lambda: greet({"dy": y + 1}))
    corners = [(e, w) for e in range(2) for w in range(2)]
    to_corner = {(e, w): {"dx": x + (1, -1)[w], "dy": y + (1, -1)[e]} for e, w in corners}
    gives_corner = {(e, w): jnp.logical_and((has_e, has_w)[w], (has_n, has_s)[e]) for e, w in corners}
    takes_corner = {(e, w): jnp.logical_and((has_w, has_e)[w], (has_s, has_n)[e]) for e, w in corners}
    for key in corners:
        pl.when(gives_corner[key])(lambda key=key: greet(to_corner[key]))

    level = lax.broadcasted_iota(jnp.int32, TILE, 0)
    lane = lax.broadcasted_iota(jnp.int32, TILE, 1)
    level_f = level.astype(F32)
    zero = jnp.zeros(TILE, F32)

    for load in loads:
        load.wait()
    weight = F32(0.0)
    for rank in range(members):
        value = 2.0 * (members - rank) / (members * (members + 1.0))
        weight = weight + jnp.where(owner[rank] == me, F32(value), F32(0.0))

    def first(r, carry):
        for f in range(FIELDS):
            state = pv[pl.ds(f * LEV * ROWS + r, LEV, stride=ROWS), :]
            other = cv[pl.ds(f * LEV * ROWS + r, LEV, stride=ROWS), :]
            s0[r + WIDTH, f] = state
            q[r, f] = weight * other - (1.0 / members) * state
        return carry

    lax.fori_loop(0, WIDTH, first, 0, unroll=2)
    lax.fori_loop(ROWS - WIDTH, ROWS, first, 0, unroll=2)
    pl.semaphore_wait(
        barrier,
        chips + sum(there.astype(jnp.int32) for there in (has_w, has_e, has_s, has_n, *takes_corner.values())),
    )

    def dd(kind, d):
        rows = pl.ds(own_b(kind, peer(d)) - WIDTH, part)
        return remote(q.at[rows, theirs], qr.at[rows], out_s, dd_r.at[d] if kind == 0 else dm_r, partner)

    def p_halo(side):
        src, dst, step = ((WIDTH, WIDTH + ROWS, -1), (ROWS, 0, 1))[side]
        return remote(
            s0.at[pl.ds(src, WIDTH), pl.ds(0, FIELDS)], s0.at[pl.ds(dst, WIDTH), pl.ds(0, FIELDS)],
            ph_s.at[side], ph_r.at[side], {"dx": x + step},
        )

    def mt_halo(side):
        return remote(mts.at[side], mtr.at[side], mt_s.at[side], mt_r.at[side], {"dx": x + (-1, 1)[side]})

    def rs(kind, d):
        return remote(
            t.at[pl.ds(own_b(kind, peer(d)) - WIDTH, part)], rr.at[kind, pl.ds((d - 1) * part, part)],
            out_s, rs_r.at[kind], same_core(d),
        )

    def swap_and_send(kind):
        if kind == 1:
            arrived(qr.at[pl.ds(WIDTH, ROWS // 2)], dm_r)
        for d in order:
            if kind == 0:
                dd(kind, d).wait_recv()
            b = own_b(kind, peer(d)) - WIDTH
            for n in range(part):
                for f in range(HALF):
                    t[b + n, f] = q[b + n, HALF * core + f] + qr[b + n, f]
            if d:
                rs(kind, d).start()

    for d in order:
        dd(0, d).start()
    pl.when(has_w)(lambda: p_halo(0).start())
    pl.when(has_e)(lambda: p_halo(1).start())
    lax.fori_loop(WIDTH, ROWS - WIDTH, first, 0, unroll=2)
    for d in order:
        dd(1, d).start()
    swap_and_send(0)
    swap_and_send(1)

    for side, start in ((0, 0), (1, ROWS - WIDTH)):
        mts[side, pl.ds(0, WIDTH), :] = mv[pl.ds(start, WIDTH), :]
        mts[side, pl.ds(WIDTH, WIDTH), :] = tv[pl.ds(start, WIDTH), :].astype(F32)
    for side, there in ((0, has_w), (1, has_e)):
        pl.when(there)(lambda side=side: mt_halo(side).start())
        sent.append(lambda side=side, there=there: pl.when(there)(mt_halo(side).wait_send))

    quad = lax.div(lane, WIDTH)

    def p_corner(e, w):
        return remote(pcs.at[e, w], pcr.at[e, w], pc_s.at[e, w], pc_r.at[e, w], to_corner[e, w])

    for e, w in corners:
        packed = zero
        for f in range(FIELDS):
            for k in range(WIDTH):
                place = f * 2 * WIDTH + w * WIDTH + k
                row = s0[(ROWS, WIDTH)[w] + k, f]
                packed = jnp.where(quad == place, pltpu.roll(row, (place + 1 - e) * WIDTH % COLS, 1), packed)
        pcs[e, w] = packed
        pl.when(gives_corner[e, w])(lambda e=e, w=w: p_corner(e, w).start())
        sent.append(lambda e=e, w=w: pl.when(gives_corner[e, w])(p_corner(e, w).wait_send))

        def no_corner(e=e, w=w):
            pcr[e, w] = zero

        pl.when(jnp.logical_not(takes_corner[e, w]))(no_corner)

    def factors(r, carry):
        s0[r + WIDTH, METRIC] = jnp.broadcast_to(mv[pl.ds(r, 1), :] * (-0.5 * integration_step), TILE)
        ground = jnp.broadcast_to(tv[pl.ds(r, 1), :], TILE)
        s0[r + WIDTH, MASK] = (level >= ground).astype(F32)
        return carry

    lax.fori_loop(0, ROWS, factors, 0)

    def empty(b0, side):
        def body():
            for b in range(WIDTH):
                for f in range(FIELDS):
                    s0[b0 + b, f] = zero
                    dx_rows[b0 + b, f] = zero
            mtr[side, pl.ds(0, WIDTH), :] = jnp.ones((WIDTH, COLS), F32)
            mtr[side, pl.ds(WIDTH, WIDTH), :] = jnp.full((WIDTH, COLS), F32(2 * LEV))
            for n in range(chips):
                cs[side * chips + n] = zero
        return body

    pl.when(jnp.logical_not(has_w))(empty(0, 1))
    pl.when(jnp.logical_not(has_e))(empty(WIDTH + ROWS, 0))

    def no_edge(side):
        def body():
            for f in range(FIELDS + 2):
                er[side, f] = zero
            crr[side] = zero
        return body

    pl.when(jnp.logical_not(has_s))(no_edge(0))
    pl.when(jnp.logical_not(has_n))(no_edge(1))

    at = x + 2 * top(chip) - 1
    gives = jnp.logical_and(at >= 0, at < nx)
    takes = came_from(chip)
    halo_here = pl.ds(halo_b(chip), part)
    hx = remote(
        dx_rows.at[pl.ds(own_b(0, chip), part), mine], dx_rows.at[halo_here, mine], hx_s, hx_r, {"dx": at}
    )

    def ag(kind, d):
        rows = pl.ds(own_b(kind, chip), part)
        return remote(
            dx_rows.at[rows, mine], dx_rows.at[rows, mine], out_s, ag_r.at[d - 1], same_core(d)
        )

    def fw(kind, d):
        rows = pl.ds(own_b(kind, source(d)), part)
        return remote(dx_rows.at[rows, mine], dx_rows.at[rows, mine], out_s, fw_r, partner)

    def ha(d):
        return remote(
            dx_rows.at[halo_here, mine], dx_rows.at[halo_here, mine], ha_s, ha_r.at[d - 1], same_core(d)
        )

    def hf(d):
        rows = pl.ds(halo_b(source(d)), part)
        return remote(dx_rows.at[rows, mine], dx_rows.at[rows, mine], hf_s.at[top(source(d))], hf_r.at[top(source(d))], partner)

    def d_corner(e):
        return remote(dcs.at[e], crr.at[e], dc_s.at[e], dc_r.at[e], {"dx": at, "dy": y + (1, -1)[e]})

    def cc(member):
        return remote(crm, cs.at[me], cs_s, cs_r.at[top(chip)], {"member": member})

    own_cc = pltpu.make_async_copy(crm, cs.at[me], cs_r.at[top(chip)])

    for kind in range(2):
        b = own_b(kind, chip)
        total = [[t[b - WIDTH + n, f] for f in range(HALF)] for n in range(part)]
        arrived(rr.at[kind], rs_r.at[kind])
        for d in near_first:
            for n in range(part):
                for f in range(HALF):
                    total[n][f] = total[n][f] + rr[kind, (d - 1) * part + n, f]
        for n in range(part):
            for f in range(HALF):
                dx_rows[b + n, HALF * core + f] = total[n][f]
        if kind == 0:
            pl.when(gives)(hx.start)
            north, south = zero, zero
            for n in range(part):
                for f in range(HALF):
                    place = (HALF * core + f) * 2 * WIDTH + chip * part + n + WIDTH - 2 * WIDTH * top(chip)
                    other = lax.rem(place + 16, 32)
                    north = jnp.where(quad == place, pltpu.roll(total[n][f], lax.rem(place + 1, 32) * WIDTH, 1), north)
                    south = jnp.where(quad == other, pltpu.roll(total[n][f], other * WIDTH, 1), south)
            dcs[0] = north
            dcs[1] = south
            for e, there in ((0, has_n), (1, has_s)):
                going = jnp.logical_and(gives, there)
                pl.when(going)(lambda e=e: d_corner(e).start())
                sent.append(lambda e=e, going=going: pl.when(going)(d_corner(e).wait_send))
            sent.append(lambda: pl.when(gives)(hx.wait_send))
        for d in far_first:
            ag(kind, d).start()
        fw(kind, 0).start()

    def spread_halo():
        hx.wait_recv()
        for d in far_first:
            ha(d).start()
        hf(0).start()

    pl.when(takes)(spread_halo)

    sent.append(lambda: pl.when(takes)(lambda: arrived(rr.at[0], ha_s)))
    def gather(ds):
        for d in ds:
            arrived(dx_rows.at[pl.ds(0, 2 * part), mine], ag_r.at[d - 1])
            for kind in range(2):
                fw(kind, d).start()

    gather(near_first[: chips // 2])

    def spread_corner():
        for e, there in ((0, has_s), (1, has_n)):
            pl.when(there)(lambda e=e: d_corner(e).wait_recv())
        crm[...] = crr[0] + crr[1]
        own_cc.start()
        for d in far_first:
            for co in range(2):
                cc(2 * peer(d) + co).start()
        cc(me + 1 - 2 * core).start()

    pl.when(takes)(spread_corner)
    sent.append(lambda: pl.when(takes)(lambda: arrived(cs.at[pl.ds(0, members - 1)], cs_s)))
    gather(near_first[chips // 2 :])
    arrived(dx_rows.at[pl.ds(0, ROWS), mine], fw_r)

    pl.when(has_w)(lambda: p_halo(0).wait_send())
    pl.when(has_e)(lambda: p_halo(1).wait_send())

    def begin(b, carry):
        for f in range(FIELDS):
            s0[b, f] = s0[b, f] + dx_rows[b, f]
        return carry

    lax.fori_loop(WIDTH, WIDTH + ROWS, begin, 0, unroll=2)
    states = (s0, s1, s2, s3, s4)
    for step in range(1, STEPS + 1):
        def row(b, carry, src=states[step - 1], dst=states[step]):
            stencil(src, dst, b, s0[b, METRIC], s0[b, MASK], level)
            return carry

        lax.fori_loop(WIDTH + step, WIDTH + ROWS - step, row, 0, unroll=True)

    inner = lax.rem(lane, 16)
    block = lax.div(lane, 16)

    def pack_rows(rows, old):
        def body(f, carry):
            for i in range(STRIP):
                groups = [g for g in range(GROUPS) if g * STRIP + i in rows]
                if not groups:
                    continue
                packed = a0[i + 1, f] if old else zero
                for g in groups:
                    row = s0[g * STRIP + i, f]
                    left = jnp.logical_and(block == g, inner >= WIDTH)
                    right = jnp.logical_and(block == GROUPS + g, inner < 16 - WIDTH)
                    packed = jnp.where(left, pltpu.roll(row, 16 * g + WIDTH, 1), packed)
                    packed = jnp.where(right, pltpu.roll(row, 16 * g + 76, 1), packed)
                a0[i + 1, f] = packed
            return carry
        return body

    inside = range(WIDTH, WIDTH + ROWS)
    outside = [b for b in range(TALL) if b not in inside]
    lax.fori_loop(0, FIELDS + 2, pack_rows(inside, False), 0)

    def halo_factors(side, b0):
        for b in range(WIDTH):
            s0[b0 + b, METRIC] = jnp.broadcast_to(mtr[side, pl.ds(b, 1), :] * (-0.5 * integration_step), TILE)
            ground = jnp.broadcast_to(mtr[side, pl.ds(WIDTH + b, 1), :], TILE)
            s0[b0 + b, MASK] = (level_f >= ground).astype(F32)

    pl.when(has_e)(lambda: mt_halo(0).wait_recv())
    pl.when(has_w)(lambda: mt_halo(1).wait_recv())
    halo_factors(0, WIDTH + ROWS)
    halo_factors(1, 0)
    lax.fori_loop(FIELDS, FIELDS + 2, pack_rows(outside, True), 0)

    for f in range(FIELDS + 2):
        north, south = zero, zero
        for i in range(STRIP):
            strip = a0[i + 1, f]
            at_lane = (i // 4) * 64 + (i % 4) * 4
            slot = jnp.logical_and(lax.div(lane, 64) == i // 4, lax.div(inner, 4) == i % 4)
            north = jnp.where(slot, pltpu.roll(strip, (at_lane - 72) % COLS, 1), north)
            south = jnp.where(slot, pltpu.roll(strip, (at_lane - 4) % COLS, 1), south)
        es[0, f] = north
        es[1, f] = south

    def edge(side):
        return remote(es.at[side], er.at[side], ed_s.at[side], ed_r.at[side], {"dy": y + (1, -1)[side]})

    for side, there in ((0, has_n), (1, has_s)):
        pl.when(there)(lambda side=side: edge(side).start())
        sent.append(lambda side=side, there=there: pl.when(there)(edge(side).wait_send))

    for d in near_first:
        def pass_on(d=d):
            ha(d).wait_recv()
            hf(d).start()

        pl.when(came_from(source(d)))(pass_on)
    pl.when(has_s)(lambda: edge(0).wait_recv())
    pl.when(has_n)(lambda: edge(1).wait_recv())
    for i in range(STRIP):
        at_lane = (i // 4) * 64 + (i % 4) * 4
        left = jnp.logical_and(block < GROUPS, inner < WIDTH)
        right = jnp.logical_and(block >= GROUPS, inner >= 16 - WIDTH)
        for f in range(FIELDS + 2):
            strip = a0[i + 1, f]
            strip = jnp.where(left, pltpu.roll(er[0, f], (-at_lane) % COLS, 1), strip)
            strip = jnp.where(right, pltpu.roll(er[1, f], (76 - at_lane) % COLS, 1), strip)
            a0[i + 1, f] = strip
    for side, there in ((0, has_e), (1, has_w)):
        rows = dx_rows.at[pl.ds(0, WIDTH), mine]
        pl.when(there)(lambda side=side, rows=rows: arrived(rows, hf_r.at[side]))
        sent.append(lambda side=side, there=there, rows=rows: pl.when(there)(lambda: arrived(rows, hf_s.at[side])))
    pl.when(has_e)(lambda: p_halo(0).wait_recv())
    pl.when(has_w)(lambda: p_halo(1).wait_recv())
    lax.fori_loop(0, WIDTH, begin, 0, unroll=2)
    lax.fori_loop(WIDTH + ROWS, TALL, begin, 0, unroll=2)

    lax.fori_loop(0, FIELDS, pack_rows(outside, True), 0)

    for step in range(1, STEPS + 1):
        def rows(j, carry, src=states[step - 1], dst=states[step], step=step):
            for b in (step + j, WIDTH + ROWS - step + j):
                stencil(src, dst, b, s0[b, METRIC], s0[b, MASK], level)
            return carry

        lax.fori_loop(0, WIDTH, rows, 0, unroll=True)

    for e, w in corners:
        pl.when(takes_corner[e, w])(lambda e=e, w=w: p_corner(e, w).wait_recv())
    for side, there in ((0, has_e), (1, has_w)):
        pl.when(there)(lambda side=side: arrived(cs.at[pl.ds(side * chips, chips)], cs_r.at[side]))
    by_core = [functools.reduce(jnp.add, [cs[2 * ch + co] for ch in range(chips)]) for co in range(2)]
    low = lane < COLS // 2
    from_south = jnp.where(low, by_core[0], by_core[1]) + (pcr[0, 0] + pcr[0, 1])
    from_north = pltpu.roll(jnp.where(low, by_core[1], by_core[0]), COLS // 2, 1) + (pcr[1, 0] + pcr[1, 1])
    for n, b in enumerate(outside):
        g, i = divmod(b, STRIP)
        left = jnp.logical_and(block == g, inner < WIDTH)
        right = jnp.logical_and(block == GROUPS + g, inner >= 16 - WIDTH)
        for f in range(FIELDS):
            at_lane = f * 32 + n * WIDTH
            strip = a0[i + 1, f]
            strip = jnp.where(left, pltpu.roll(from_south, (16 * g - at_lane) % COLS, 1), strip)
            strip = jnp.where(right, pltpu.roll(from_north, (76 + 16 * g - at_lane) % COLS, 1), strip)
            a0[i + 1, f] = strip
    for step in range(STEPS):
        src, dst = (a0, a1) if step % 2 == 0 else (a1, a0)
        for f in range(FIELDS):
            src[0, f] = pltpu.roll(src[STRIP, f], 16, 1)
            src[STRIP + 1, f] = pltpu.roll(src[1, f], COLS - 16, 1)

        def strip_row(i, carry, src=src, dst=dst):
            stencil(src, dst, i, a0[i, METRIC], a0[i, MASK], level)
            return carry

        lax.fori_loop(1, STRIP + 1, strip_row, 0, unroll=True)

    for g in range(GROUPS):
        def merge(i, carry, g=g):
            for f in range(FIELDS):
                strip = a0[i + 1, f]
                new = s4[g * STRIP + i, f]
                new = jnp.where(lane < WIDTH, pltpu.roll(strip, (-16 * g - WIDTH) % COLS, 1), new)
                new = jnp.where(lane >= COLS - WIDTH, pltpu.roll(strip, (52 - 16 * g) % COLS, 1), new)
                out[pl.ds(f * LEV * ROWS + g * STRIP + i - WIDTH, LEV, stride=ROWS), :] = new
            return carry

        lax.fori_loop(max(0, WIDTH - g * STRIP), min(STRIP, WIDTH + ROWS - g * STRIP), merge, 0, unroll=True)
    arrived(s0.at[pl.ds(0, pieces * part * HALF // (FIELDS + 2))], out_s)
    for wait in sent:
        wait()


def solution(mesh):
    members, nx, ny = (mesh.shape[axis] for axis in ("member", "dx", "dy"))
    chips = members // 2
    part = (ROWS // 2) // chips
    flat = FIELDS * LEV * ROWS

    def on_device(states, control, owner, map_factor, terrain):
        any_space = pl.BlockSpec(memory_space=pl.ANY)
        dma = pltpu.SemaphoreType.DMA
        out = pl.pallas_call(
            functools.partial(kernel, members, nx, ny),
            out_shape=pltpu.VMEM((flat, COLS), F32),
            in_specs=[any_space] * 5,
            out_specs=pl.BlockSpec(memory_space=pltpu.VMEM),
            scratch_shapes=[
                pltpu.VMEM((flat, COLS), F32),
                pltpu.VMEM((flat, COLS), F32),
                pltpu.SMEM((members,), jnp.int32),
                pltpu.VMEM((ROWS, COLS), F32),
                pltpu.VMEM((ROWS, COLS), jnp.int32),
                pltpu.VMEM((TALL, FIELDS + 2) + TILE, F32),
                pltpu.VMEM((TALL, FIELDS) + TILE, F32),
                pltpu.VMEM((TALL, FIELDS) + TILE, F32),
                pltpu.VMEM((TALL, FIELDS) + TILE, F32),
                pltpu.VMEM((TALL, FIELDS) + TILE, F32),
                pltpu.VMEM((ROWS, FIELDS) + TILE, F32),
                pltpu.VMEM((ROWS, HALF) + TILE, F32),
                pltpu.VMEM((ROWS, HALF) + TILE, F32),
                pltpu.VMEM((2, part * (chips - 1), HALF) + TILE, F32),
                pltpu.VMEM((TALL, FIELDS) + TILE, F32),
                pltpu.VMEM((2,) + TILE, F32),
                pltpu.VMEM((2,) + TILE, F32),
                pltpu.VMEM((STRIP + 2, FIELDS + 2) + TILE, F32),
                pltpu.VMEM((STRIP + 2, FIELDS) + TILE, F32),
                pltpu.VMEM((2, FIELDS + 2) + TILE, F32),
                pltpu.VMEM((2, FIELDS + 2) + TILE, F32),
                pltpu.VMEM((2, 2) + TILE, F32),
                pltpu.VMEM((2, 2) + TILE, F32),
                pltpu.VMEM((2,) + TILE, F32),
                pltpu.VMEM((2,) + TILE, F32),
                pltpu.VMEM(TILE, F32),
                pltpu.VMEM((members,) + TILE, F32),
                dma((5,)),
                dma, dma((chips,)), dma, dma((2,)), dma((chips - 1,)), dma,
                dma, dma,
                dma, dma((chips - 1,)),
                dma((2,)), dma((2,)),
                dma((2,)), dma((2,)),
                dma((2,)), dma((2,)),
                dma((2,)), dma((2,)),
                dma((2, 2)), dma((2, 2)),
                dma((2,)), dma((2,)),
                dma, dma((2,)),
            ],
            compiler_params=pltpu.CompilerParams(collective_id=0, has_side_effects=True),
        )(states.reshape(flat, COLS), control.reshape(flat, COLS), owner, map_factor, terrain)
        return out.reshape(states.shape)

    spread = P("member", None, None, "dx", "dy")
    return jax.shard_map(
        on_device,
        mesh=mesh,
        in_specs=(spread, spread, P(), P("dx", "dy"), P("dx", "dy")),
        out_specs=spread,
        check_vma=False,
    )
```

```python
import functools

import jax
import jax.numpy as jnp
from jax import lax
from jax.experimental import pallas as pl
from jax.experimental.pallas import tpu as pltpu
from jax.sharding import PartitionSpec as P

MESH = pl.DeviceIdType.MESH
F32 = jnp.float32

STEPS = 4
FIELDS = 4
HALF = FIELDS // 2
LEV = 8
ROWS = 16
COLS = 128
WIDTH = STEPS
TALL = ROWS + 2 * WIDTH
GROUPS = 4
STRIP = TALL // GROUPS
METRIC, MASK = FIELDS, FIELDS + 1
TILE = (LEV, COLS)

integration_step = 0.2
diffusion = 0.1


def stencil(src, dst, b, metric, mask, level):
    mid = [src[b, f] for f in range(FIELDS)]
    east = [src[b + 1, f] for f in range(FIELDS)]
    west = [src[b - 1, f] for f in range(FIELDS)]
    along_x = metric * mid[0]
    along_y = metric * mid[1]
    new, gx, gy = [], [], []
    for f in range(FIELDS):
        north = pltpu.roll(mid[f], COLS - 1, 1)
        south = pltpu.roll(mid[f], 1, 1)
        above = jnp.where(level < LEV - 1, pltpu.roll(mid[f], LEV - 1, 0), 0.0)
        below = jnp.where(level > 0, pltpu.roll(mid[f], 1, 0), 0.0)
        gx.append(east[f] - west[f])
        gy.append(north - south)
        six = (east[f] + west[f]) + (north + south) + (above + below)
        flow = along_x * gx[f] + along_y * gy[f]
        rate = integration_step * diffusion
        new.append((1.0 - 6.0 * rate) * mid[f] + rate * six + flow)
    new[0] = new[0] + metric * gx[2]
    new[1] = new[1] + metric * gy[2]
    new[2] = new[2] + metric * (gx[0] + gy[1])
    for f in range(FIELDS):
        dst[b, f] = mask * new[f]


def kernel(
    members, nx, ny,
    p_hbm, c_hbm, owner_hbm, map_hbm, ter_hbm, out,
    pv, cv, owner, mv, tv, s0, s1, s2, s3, s4, q, qr, t, rr, dx_rows, mts, mtr, a0, a1, es, er, pcs, pcr, dcs, crr, crm, cs,
    local_sem, out_s, dd_r, dm_r, rs_r, ag_r, fw_r, hx_s, hx_r, ha_s, ha_r, hf_s, hf_r,
    ph_s, ph_r, mt_s, mt_r, ed_s, ed_r, pc_s, pc_r, dc_s, dc_r, cs_s, cs_r,
):
    chips = members // 2
    part = (ROWS // 2) // chips
    me = lax.axis_index("member")
    x = lax.axis_index("dx")
    y = lax.axis_index("dy")
    chip = lax.div(me, 2)
    core = lax.rem(me, 2)
    partner = {"member": me + 1 - 2 * core}
    has_w, has_e = x > 0, x < nx - 1
    has_s, has_n = y > 0, y < ny - 1
    far_first = sorted(range(1, chips), key=lambda d: -min(d, chips - d))
    near_first = far_first[::-1]
    order = far_first + [0]
    direct = [d for d in far_first if min(d, chips - d) > 2]
    mine = pl.ds(HALF * core, HALF)
    theirs = pl.ds(HALF * (1 - core), HALF)
    sent = []
    pieces = 2 * chips + 2 * (chips - 1) + 2 * (chips - 1) + 2 * chips

    def peer(d):
        return lax.rem(chip + d, chips)

    def source(d):
        return lax.rem(chip + chips - d, chips)

    def top(ch):
        return lax.div(2 * ch, chips)

    def own_b(kind, ch):
        if kind == 0:
            return WIDTH + ch * part + (ROWS // 2) * top(ch)
        return 2 * WIDTH + ch * part

    def halo_b(ch):
        return ch * part + (WIDTH + ROWS) - TALL * top(ch)

    def came_from(ch):
        at = x + 1 - 2 * top(ch)
        return jnp.logical_and(at >= 0, at < nx)

    def remote(src, dst, ss, rs, device):
        return pltpu.make_async_remote_copy(
            src_ref=src, dst_ref=dst, send_sem=ss, recv_sem=rs, device_id=device, device_id_type=MESH
        )

    def arrived(ref, sem):
        pltpu.make_async_copy(ref, ref, sem).wait()

    def same_core(d):
        return {"member": 2 * peer(d) + core}

    loads = [
        pltpu.make_async_copy(p_hbm, pv, local_sem.at[0]),
        pltpu.make_async_copy(c_hbm, cv, local_sem.at[1]),
        pltpu.make_async_copy(owner_hbm, owner, local_sem.at[2]),
        pltpu.make_async_copy(map_hbm, mv, local_sem.at[3]),
        pltpu.make_async_copy(ter_hbm, tv, local_sem.at[4]),
    ]
    for load in loads:
        load.start()
    barrier = pltpu.get_barrier_semaphore()

    def greet(device):
        pl.semaphore_signal(barrier, inc=1, device_id=device, device_id_type=MESH)

    pl.when(has_w)(lambda: greet({"dx": x - 1}))
    pl.when(has_e)(lambda: greet({"dx": x + 1}))
    for d in far_first:
        greet(same_core(d))
    greet(partner)
    pl.when(has_s)(lambda: greet({"dy": y - 1}))
    pl.when(has_n)(lambda: greet({"dy": y + 1}))
    corners = [(e, w) for e in range(2) for w in range(2)]
    to_corner = {(e, w): {"dx": x + (1, -1)[w], "dy": y + (1, -1)[e]} for e, w in corners}
    gives_corner = {(e, w): jnp.logical_and((has_e, has_w)[w], (has_n, has_s)[e]) for e, w in corners}
    takes_corner = {(e, w): jnp.logical_and((has_w, has_e)[w], (has_s, has_n)[e]) for e, w in corners}
    for key in corners:
        pl.when(gives_corner[key])(lambda key=key: greet(to_corner[key]))

    level = lax.broadcasted_iota(jnp.int32, TILE, 0)
    lane = lax.broadcasted_iota(jnp.int32, TILE, 1)
    level_f = level.astype(F32)
    zero = jnp.zeros(TILE, F32)

    for load in loads:
        load.wait()
    weight = F32(0.0)
    for rank in range(members):
        value = 2.0 * (members - rank) / (members * (members + 1.0))
        weight = weight + jnp.where(owner[rank] == me, F32(value), F32(0.0))

    def first(r, carry):
        for f in range(FIELDS):
            state = pv[pl.ds(f * LEV * ROWS + r, LEV, stride=ROWS), :]
            other = cv[pl.ds(f * LEV * ROWS + r, LEV, stride=ROWS), :]
            s0[r + WIDTH, f] = state
            q[r, f] = weight * other - (1.0 / members) * state
        return carry

    lax.fori_loop(0, WIDTH, first, 0, unroll=2)
    lax.fori_loop(ROWS - WIDTH, ROWS, first, 0, unroll=2)
    pl.semaphore_wait(
        barrier,
        chips + sum(there.astype(jnp.int32) for there in (has_w, has_e, has_s, has_n, *takes_corner.values())),
    )

    def dd(kind, d):
        rows = pl.ds(own_b(kind, peer(d)) - WIDTH, part)
        return remote(q.at[rows, theirs], qr.at[rows], out_s, dd_r.at[d] if kind == 0 else dm_r, partner)

    def p_halo(side):
        src, dst, step = ((WIDTH, WIDTH + ROWS, -1), (ROWS, 0, 1))[side]
        return remote(
            s0.at[pl.ds(src, WIDTH), pl.ds(0, FIELDS)], s0.at[pl.ds(dst, WIDTH), pl.ds(0, FIELDS)],
            ph_s.at[side], ph_r.at[side], {"dx": x + step},
        )

    def mt_halo(side):
        return remote(mts.at[side], mtr.at[side], mt_s.at[side], mt_r.at[side], {"dx": x + (-1, 1)[side]})

    def rs(kind, d):
        return remote(
            t.at[pl.ds(own_b(kind, peer(d)) - WIDTH, part)], rr.at[kind, pl.ds((d - 1) * part, part)],
            out_s, rs_r.at[kind], same_core(d),
        )

    def swap_and_send(kind):
        if kind == 1:
            arrived(qr.at[pl.ds(WIDTH, ROWS // 2)], dm_r)
        for d in order:
            if kind == 0:
                dd(kind, d).wait_recv()
            b = own_b(kind, peer(d)) - WIDTH
            for n in range(part):
                for f in range(HALF):
                    t[b + n, f] = q[b + n, HALF * core + f] + qr[b + n, f]
            if d:
                rs(kind, d).start()

    for d in order:
        dd(0, d).start()
    pl.when(has_w)(lambda: p_halo(0).start())
    pl.when(has_e)(lambda: p_halo(1).start())
    lax.fori_loop(WIDTH, ROWS - WIDTH, first, 0, unroll=2)
    for d in order:
        dd(1, d).start()
    swap_and_send(0)
    swap_and_send(1)

    for side, start in ((0, 0), (1, ROWS - WIDTH)):
        mts[side, pl.ds(0, WIDTH), :] = mv[pl.ds(start, WIDTH), :]
        mts[side, pl.ds(WIDTH, WIDTH), :] = tv[pl.ds(start, WIDTH), :].astype(F32)
    for side, there in ((0, has_w), (1, has_e)):
        pl.when(there)(lambda side=side: mt_halo(side).start())
        sent.append(lambda side=side, there=there: pl.when(there)(mt_halo(side).wait_send))

    quad = lax.div(lane, WIDTH)

    def p_corner(e, w):
        return remote(pcs.at[e, w], pcr.at[e, w], pc_s.at[e, w], pc_r.at[e, w], to_corner[e, w])

    for e, w in corners:
        packed = zero
        for f in range(FIELDS):
            for k in range(WIDTH):
                place = f * 2 * WIDTH + w * WIDTH + k
                row = s0[(ROWS, WIDTH)[w] + k, f]
                packed = jnp.where(quad == place, pltpu.roll(row, (place + 1 - e) * WIDTH % COLS, 1), packed)
        pcs[e, w] = packed
        pl.when(gives_corner[e, w])(lambda e=e, w=w: p_corner(e, w).start())
        sent.append(lambda e=e, w=w: pl.when(gives_corner[e, w])(p_corner(e, w).wait_send))

        def no_corner(e=e, w=w):
            pcr[e, w] = zero

        pl.when(jnp.logical_not(takes_corner[e, w]))(no_corner)

    def factors(r, carry):
        s0[r + WIDTH, METRIC] = jnp.broadcast_to(mv[pl.ds(r, 1), :] * (-0.5 * integration_step), TILE)
        ground = jnp.broadcast_to(tv[pl.ds(r, 1), :], TILE)
        s0[r + WIDTH, MASK] = (level >= ground).astype(F32)
        return carry

    lax.fori_loop(0, ROWS, factors, 0)

    def empty(b0, side):
        def body():
            for b in range(WIDTH):
                for f in range(FIELDS):
                    s0[b0 + b, f] = zero
                    dx_rows[b0 + b, f] = zero
            mtr[side, pl.ds(0, WIDTH), :] = jnp.ones((WIDTH, COLS), F32)
            mtr[side, pl.ds(WIDTH, WIDTH), :] = jnp.full((WIDTH, COLS), F32(2 * LEV))
            for n in range(chips):
                cs[side * chips + n] = zero
        return body

    pl.when(jnp.logical_not(has_w))(empty(0, 1))
    pl.when(jnp.logical_not(has_e))(empty(WIDTH + ROWS, 0))

    def no_edge(side):
        def body():
            for f in range(FIELDS + 2):
                er[side, f] = zero
            crr[side] = zero
        return body

    pl.when(jnp.logical_not(has_s))(no_edge(0))
    pl.when(jnp.logical_not(has_n))(no_edge(1))

    at = x + 2 * top(chip) - 1
    gives = jnp.logical_and(at >= 0, at < nx)
    takes = came_from(chip)
    halo_here = pl.ds(halo_b(chip), part)
    hx = remote(
        dx_rows.at[pl.ds(own_b(0, chip), part), mine], dx_rows.at[halo_here, mine], hx_s, hx_r, {"dx": at}
    )

    def ag(kind, d):
        rows = pl.ds(own_b(kind, chip), part)
        return remote(
            dx_rows.at[rows, mine], dx_rows.at[rows, mine], out_s, ag_r.at[d - 1], same_core(d)
        )

    def fw(kind, d):
        rows = pl.ds(own_b(kind, source(d)), part)
        return remote(dx_rows.at[rows, mine], dx_rows.at[rows, mine], out_s, fw_r, partner)

    def ha(d):
        return remote(
            dx_rows.at[halo_here, mine], dx_rows.at[halo_here, mine], ha_s, ha_r.at[d - 1], same_core(d)
        )

    def both(d):
        rows = dx_rows.at[halo_here, mine]
        return remote(rows, rows, ha_s, hf_r.at[top(chip)], {"member": 2 * peer(d) + 1 - core})

    def hf(d):
        rows = pl.ds(halo_b(source(d)), part)
        return remote(dx_rows.at[rows, mine], dx_rows.at[rows, mine], hf_s.at[d], hf_r.at[top(source(d))], partner)

    def d_corner(e):
        return remote(dcs.at[e], crr.at[e], dc_s.at[e], dc_r.at[e], {"dx": at, "dy": y + (1, -1)[e]})

    def cc(member):
        return remote(crm, cs.at[me], cs_s, cs_r.at[top(chip)], {"member": member})

    own_cc = pltpu.make_async_copy(crm, cs.at[me], cs_r.at[top(chip)])

    for kind in range(2):
        b = own_b(kind, chip)
        total = [[t[b - WIDTH + n, f] for f in range(HALF)] for n in range(part)]
        arrived(rr.at[kind], rs_r.at[kind])
        for d in near_first:
            for n in range(part):
                for f in range(HALF):
                    total[n][f] = total[n][f] + rr[kind, (d - 1) * part + n, f]
        for n in range(part):
            for f in range(HALF):
                dx_rows[b + n, HALF * core + f] = total[n][f]
        if kind == 0:
            pl.when(gives)(hx.start)
            north, south = zero, zero
            for n in range(part):
                for f in range(HALF):
                    place = (HALF * core + f) * 2 * WIDTH + chip * part + n + WIDTH - 2 * WIDTH * top(chip)
                    other = lax.rem(place + 16, 32)
                    north = jnp.where(quad == place, pltpu.roll(total[n][f], lax.rem(place + 1, 32) * WIDTH, 1), north)
                    south = jnp.where(quad == other, pltpu.roll(total[n][f], other * WIDTH, 1), south)
            dcs[0] = north
            dcs[1] = south
            for e, there in ((0, has_n), (1, has_s)):
                going = jnp.logical_and(gives, there)
                pl.when(going)(lambda e=e: d_corner(e).start())
                sent.append(lambda e=e, going=going: pl.when(going)(d_corner(e).wait_send))
            sent.append(lambda: pl.when(gives)(hx.wait_send))
        for d in far_first:
            ag(kind, d).start()
        fw(kind, 0).start()

    inner = lax.rem(lane, 16)
    block = lax.div(lane, 16)

    def pack_rows(rows, old):
        def body(f, carry):
            for i in range(STRIP):
                groups = [g for g in range(GROUPS) if g * STRIP + i in rows]
                if not groups:
                    continue
                packed = a0[i + 1, f] if old else zero
                for g in groups:
                    row = s0[g * STRIP + i, f]
                    left = jnp.logical_and(block == g, inner >= WIDTH)
                    right = jnp.logical_and(block == GROUPS + g, inner < 16 - WIDTH)
                    packed = jnp.where(left, pltpu.roll(row, 16 * g + WIDTH, 1), packed)
                    packed = jnp.where(right, pltpu.roll(row, 16 * g + 76, 1), packed)
                a0[i + 1, f] = packed
            return carry
        return body

    inside = range(WIDTH, WIDTH + ROWS)
    outside = [b for b in range(TALL) if b not in inside]

    def halo_factors(side, b0):
        for b in range(WIDTH):
            s0[b0 + b, METRIC] = jnp.broadcast_to(mtr[side, pl.ds(b, 1), :] * (-0.5 * integration_step), TILE)
            ground = jnp.broadcast_to(mtr[side, pl.ds(WIDTH + b, 1), :], TILE)
            s0[b0 + b, MASK] = (level_f >= ground).astype(F32)

    pl.when(has_e)(lambda: mt_halo(0).wait_recv())
    pl.when(has_w)(lambda: mt_halo(1).wait_recv())
    halo_factors(0, WIDTH + ROWS)
    halo_factors(1, 0)
    lax.fori_loop(FIELDS, FIELDS + 2, pack_rows(range(TALL), False), 0, unroll=True)

    def edge(side, late):
        fields = pl.ds(0, FIELDS) if late else pl.ds(FIELDS, 2)
        k = side + 2 * late
        return remote(es.at[side, fields], er.at[side, fields], ed_s.at[k], ed_r.at[k], {"dy": y + (1, -1)[side]})

    def send_edges(late):
        for f in range(FIELDS) if late else (METRIC, MASK):
            north, south = zero, zero
            for i in range(STRIP):
                strip = a0[i + 1, f]
                at_lane = (i // 4) * 64 + (i % 4) * 4
                slot = jnp.logical_and(lax.div(lane, 64) == i // 4, lax.div(inner, 4) == i % 4)
                north = jnp.where(slot, pltpu.roll(strip, (at_lane - 72) % COLS, 1), north)
                south = jnp.where(slot, pltpu.roll(strip, (at_lane - 4) % COLS, 1), south)
            es[0, f] = north
            es[1, f] = south
        for side, there in ((0, has_n), (1, has_s)):
            pl.when(there)(lambda side=side: edge(side, late).start())
            sent.append(lambda side=side, there=there: pl.when(there)(edge(side, late).wait_send))

    send_edges(0)

    def spread_halo():
        hx.wait_recv()
        for d in far_first:
            ha(d).start()
            if d in direct:
                both(d).start()
        hf(0).start()

    pl.when(takes)(spread_halo)

    spread_bytes = q.at[pl.ds(0, (chips - 1 + len(direct)) * part * HALF // FIELDS)]
    sent.append(lambda: pl.when(takes)(lambda: arrived(spread_bytes, ha_s)))
    def gather(ds):
        for d in ds:
            arrived(dx_rows.at[pl.ds(0, 2 * part), mine], ag_r.at[d - 1])
            for kind in range(2):
                fw(kind, d).start()

    gather(near_first[: chips // 2])

    def spread_corner():
        for e, there in ((0, has_s), (1, has_n)):
            pl.when(there)(lambda e=e: d_corner(e).wait_recv())
        crm[...] = crr[0] + crr[1]
        own_cc.start()
        for d in far_first:
            for co in range(2):
                cc(2 * peer(d) + co).start()
        cc(me + 1 - 2 * core).start()

    pl.when(takes)(spread_corner)
    sent.append(lambda: pl.when(takes)(lambda: arrived(cs.at[pl.ds(0, members - 1)], cs_s)))
    gather(near_first[chips // 2 :])
    arrived(dx_rows.at[pl.ds(0, ROWS), mine], fw_r)

    pl.when(has_w)(lambda: p_halo(0).wait_send())
    pl.when(has_e)(lambda: p_halo(1).wait_send())

    def begin(b, carry):
        for f in range(FIELDS):
            s0[b, f] = s0[b, f] + dx_rows[b, f]
        return carry

    lax.fori_loop(WIDTH, WIDTH + ROWS, begin, 0, unroll=True)
    lax.fori_loop(0, FIELDS, pack_rows(inside, False), 0, unroll=True)
    send_edges(1)
    states = (s0, s1, s2, s3, s4)
    for step in range(1, STEPS + 1):
        def row(b, carry, src=states[step - 1], dst=states[step]):
            stencil(src, dst, b, s0[b, METRIC], s0[b, MASK], level)
            return carry

        lax.fori_loop(WIDTH + step, WIDTH + ROWS - step, row, 0, unroll=True)

    for d in near_first:
        def pass_on(d=d):
            ha(d).wait_recv()
            if d not in direct:
                hf(d).start()

        pl.when(came_from(source(d)))(pass_on)
    for late in range(2):
        pl.when(has_s)(lambda late=late: edge(0, late).wait_recv())
        pl.when(has_n)(lambda late=late: edge(1, late).wait_recv())
    for i in range(STRIP):
        at_lane = (i // 4) * 64 + (i % 4) * 4
        left = jnp.logical_and(block < GROUPS, inner < WIDTH)
        right = jnp.logical_and(block >= GROUPS, inner >= 16 - WIDTH)
        for f in range(FIELDS + 2):
            strip = a0[i + 1, f]
            strip = jnp.where(left, pltpu.roll(er[0, f], (-at_lane) % COLS, 1), strip)
            strip = jnp.where(right, pltpu.roll(er[1, f], (76 - at_lane) % COLS, 1), strip)
            a0[i + 1, f] = strip
    for d in range(chips):
        if d not in direct:
            sent.append(lambda d=d: pl.when(came_from(source(d)))(hf(d).wait_send))
    for side, there in ((0, has_e), (1, has_w)):
        rows = dx_rows.at[pl.ds(0, WIDTH), mine]
        pl.when(there)(lambda side=side, rows=rows: arrived(rows, hf_r.at[side]))
    pl.when(has_e)(lambda: p_halo(0).wait_recv())
    pl.when(has_w)(lambda: p_halo(1).wait_recv())
    lax.fori_loop(0, WIDTH, begin, 0, unroll=True)
    lax.fori_loop(WIDTH + ROWS, TALL, begin, 0, unroll=True)

    lax.fori_loop(0, FIELDS, pack_rows(outside, True), 0, unroll=True)

    for step in range(1, STEPS + 1):
        def rows(j, carry, src=states[step - 1], dst=states[step], step=step):
            for b in (step + j, WIDTH + ROWS - step + j):
                stencil(src, dst, b, s0[b, METRIC], s0[b, MASK], level)
            return carry

        lax.fori_loop(0, WIDTH, rows, 0, unroll=True)

    for e, w in corners:
        pl.when(takes_corner[e, w])(lambda e=e, w=w: p_corner(e, w).wait_recv())
    for side, there in ((0, has_e), (1, has_w)):
        pl.when(there)(lambda side=side: arrived(cs.at[pl.ds(side * chips, chips)], cs_r.at[side]))
    by_core = [functools.reduce(jnp.add, [cs[2 * ch + co] for ch in range(chips)]) for co in range(2)]
    low = lane < COLS // 2
    from_south = jnp.where(low, by_core[0], by_core[1]) + (pcr[0, 0] + pcr[0, 1])
    from_north = pltpu.roll(jnp.where(low, by_core[1], by_core[0]), COLS // 2, 1) + (pcr[1, 0] + pcr[1, 1])
    for n, b in enumerate(outside):
        g, i = divmod(b, STRIP)
        left = jnp.logical_and(block == g, inner < WIDTH)
        right = jnp.logical_and(block == GROUPS + g, inner >= 16 - WIDTH)
        for f in range(FIELDS):
            at_lane = f * 32 + n * WIDTH
            strip = a0[i + 1, f]
            strip = jnp.where(left, pltpu.roll(from_south, (16 * g - at_lane) % COLS, 1), strip)
            strip = jnp.where(right, pltpu.roll(from_north, (76 + 16 * g - at_lane) % COLS, 1), strip)
            a0[i + 1, f] = strip
    for step in range(STEPS):
        src, dst = (a0, a1) if step % 2 == 0 else (a1, a0)
        for f in range(FIELDS):
            src[0, f] = pltpu.roll(src[STRIP, f], 16, 1)
            src[STRIP + 1, f] = pltpu.roll(src[1, f], COLS - 16, 1)

        def strip_row(i, carry, src=src, dst=dst):
            stencil(src, dst, i, a0[i, METRIC], a0[i, MASK], level)
            return carry

        lax.fori_loop(1, STRIP + 1, strip_row, 0, unroll=True)

    for g in range(GROUPS):
        def merge(i, carry, g=g):
            for f in range(FIELDS):
                strip = a0[i + 1, f]
                new = s4[g * STRIP + i, f]
                new = jnp.where(lane < WIDTH, pltpu.roll(strip, (-16 * g - WIDTH) % COLS, 1), new)
                new = jnp.where(lane >= COLS - WIDTH, pltpu.roll(strip, (52 - 16 * g) % COLS, 1), new)
                out[pl.ds(f * LEV * ROWS + g * STRIP + i - WIDTH, LEV, stride=ROWS), :] = new
            return carry

        lax.fori_loop(max(0, WIDTH - g * STRIP), min(STRIP, WIDTH + ROWS - g * STRIP), merge, 0, unroll=True)
    arrived(s0.at[pl.ds(0, pieces * part * HALF // (FIELDS + 2))], out_s)
    for wait in sent:
        wait()


def solution(mesh):
    members, nx, ny = (mesh.shape[axis] for axis in ("member", "dx", "dy"))
    chips = members // 2
    part = (ROWS // 2) // chips
    flat = FIELDS * LEV * ROWS

    def on_device(states, control, owner, map_factor, terrain):
        any_space = pl.BlockSpec(memory_space=pl.ANY)
        dma = pltpu.SemaphoreType.DMA
        out = pl.pallas_call(
            functools.partial(kernel, members, nx, ny),
            out_shape=pltpu.VMEM((flat, COLS), F32),
            in_specs=[any_space] * 5,
            out_specs=pl.BlockSpec(memory_space=pltpu.VMEM),
            scratch_shapes=[
                pltpu.VMEM((flat, COLS), F32),
                pltpu.VMEM((flat, COLS), F32),
                pltpu.SMEM((members,), jnp.int32),
                pltpu.VMEM((ROWS, COLS), F32),
                pltpu.VMEM((ROWS, COLS), jnp.int32),
                pltpu.VMEM((TALL, FIELDS + 2) + TILE, F32),
                pltpu.VMEM((TALL, FIELDS) + TILE, F32),
                pltpu.VMEM((TALL, FIELDS) + TILE, F32),
                pltpu.VMEM((TALL, FIELDS) + TILE, F32),
                pltpu.VMEM((TALL, FIELDS) + TILE, F32),
                pltpu.VMEM((ROWS, FIELDS) + TILE, F32),
                pltpu.VMEM((ROWS, HALF) + TILE, F32),
                pltpu.VMEM((ROWS, HALF) + TILE, F32),
                pltpu.VMEM((2, part * (chips - 1), HALF) + TILE, F32),
                pltpu.VMEM((TALL, FIELDS) + TILE, F32),
                pltpu.VMEM((2,) + TILE, F32),
                pltpu.VMEM((2,) + TILE, F32),
                pltpu.VMEM((STRIP + 2, FIELDS + 2) + TILE, F32),
                pltpu.VMEM((STRIP + 2, FIELDS) + TILE, F32),
                pltpu.VMEM((2, FIELDS + 2) + TILE, F32),
                pltpu.VMEM((2, FIELDS + 2) + TILE, F32),
                pltpu.VMEM((2, 2) + TILE, F32),
                pltpu.VMEM((2, 2) + TILE, F32),
                pltpu.VMEM((2,) + TILE, F32),
                pltpu.VMEM((2,) + TILE, F32),
                pltpu.VMEM(TILE, F32),
                pltpu.VMEM((members,) + TILE, F32),
                dma((5,)),
                dma, dma((chips,)), dma, dma((2,)), dma((chips - 1,)), dma,
                dma, dma,
                dma, dma((chips - 1,)),
                dma((chips,)), dma((2,)),
                dma((2,)), dma((2,)),
                dma((2,)), dma((2,)),
                dma((4,)), dma((4,)),
                dma((2, 2)), dma((2, 2)),
                dma((2,)), dma((2,)),
                dma, dma((2,)),
            ],
            compiler_params=pltpu.CompilerParams(collective_id=0, has_side_effects=True),
        )(states.reshape(flat, COLS), control.reshape(flat, COLS), owner, map_factor, terrain)
        return out.reshape(states.shape)

    spread = P("member", None, None, "dx", "dy")
    return jax.shard_map(
        on_device,
        mesh=mesh,
        in_specs=(spread, spread, P(), P("dx", "dy"), P("dx", "dy")),
        out_specs=spread,
        check_vma=False,
    )
```

```python
import functools

import jax
import jax.numpy as jnp
from jax import lax
from jax.experimental import pallas as pl
from jax.experimental.pallas import tpu as pltpu
from jax.sharding import PartitionSpec as P

MESH = pl.DeviceIdType.MESH
F32 = jnp.float32

STEPS = 4
FIELDS = 4
HALF = FIELDS // 2
LEV = 8
ROWS = 16
COLS = 128
WIDTH = STEPS
TALL = ROWS + 2 * WIDTH
GROUPS = 4
STRIP = TALL // GROUPS
METRIC, MASK = FIELDS, FIELDS + 1
TILE = (LEV, COLS)

integration_step = 0.2
diffusion = 0.1


def stencil(src, dst, b, metric, mask, level):
    mid = [src[b, f] for f in range(FIELDS)]
    east = [src[b + 1, f] for f in range(FIELDS)]
    west = [src[b - 1, f] for f in range(FIELDS)]
    along_x = metric * mid[0]
    along_y = metric * mid[1]
    new, gx, gy = [], [], []
    for f in range(FIELDS):
        north = pltpu.roll(mid[f], COLS - 1, 1)
        south = pltpu.roll(mid[f], 1, 1)
        above = jnp.where(level < LEV - 1, pltpu.roll(mid[f], LEV - 1, 0), 0.0)
        below = jnp.where(level > 0, pltpu.roll(mid[f], 1, 0), 0.0)
        gx.append(east[f] - west[f])
        gy.append(north - south)
        six = (east[f] + west[f]) + (north + south) + (above + below)
        flow = along_x * gx[f] + along_y * gy[f]
        rate = integration_step * diffusion
        new.append((1.0 - 6.0 * rate) * mid[f] + rate * six + flow)
    new[0] = new[0] + metric * gx[2]
    new[1] = new[1] + metric * gy[2]
    new[2] = new[2] + metric * (gx[0] + gy[1])
    for f in range(FIELDS):
        dst[b, f] = mask * new[f]


def kernel(
    members, nx, ny,
    p_hbm, c_hbm, owner_hbm, map_hbm, ter_hbm, out,
    pv, cv, owner, mv, tv, s0, s1, s2, s3, s4, q, qr, t, rr, dx_rows, mts, mtr, a0, a1, es, er, pcs, pcr, dcs, crr, crm, cs, ph,
    local_sem, out_s, dd_r, dm_r, rs_r, ag_r, fw_r, hx_s, hx_r, ha_s, ha_r, hf_s, hf_r,
    ph_s, ph_r, mt_s, mt_r, ed_s, ed_r, pc_s, pc_r, dc_s, dc_r, cs_s, cs_r, hello, ready, far, ready_far,
):
    chips = members // 2
    part = (ROWS // 2) // chips
    me = lax.axis_index("member")
    x = lax.axis_index("dx")
    y = lax.axis_index("dy")
    chip = lax.div(me, 2)
    core = lax.rem(me, 2)
    partner = {"member": me + 1 - 2 * core}
    has_w, has_e = x > 0, x < nx - 1
    has_s, has_n = y > 0, y < ny - 1
    far_first = sorted(range(1, chips), key=lambda d: -min(d, chips - d))
    near_first = far_first[::-1]
    order = far_first + [0]
    direct = [d for d in far_first if min(d, chips - d) > 2]
    mine = pl.ds(HALF * core, HALF)
    theirs = pl.ds(HALF * (1 - core), HALF)
    sent = []
    pieces = 2 * chips + 2 * (chips - 1) + 2 * (chips - 1) + 2 * chips

    def peer(d):
        return lax.rem(chip + d, chips)

    def source(d):
        return lax.rem(chip + chips - d, chips)

    def top(ch):
        return lax.div(2 * ch, chips)

    def own_b(kind, ch):
        if kind == 0:
            return WIDTH + ch * part + (ROWS // 2) * top(ch)
        return 2 * WIDTH + ch * part

    def halo_b(ch):
        return ch * part + (WIDTH + ROWS) - TALL * top(ch)

    def came_from(ch):
        at = x + 1 - 2 * top(ch)
        return jnp.logical_and(at >= 0, at < nx)

    def remote(src, dst, ss, rs, device):
        return pltpu.make_async_remote_copy(
            src_ref=src, dst_ref=dst, send_sem=ss, recv_sem=rs, device_id=device, device_id_type=MESH
        )

    def arrived(ref, sem):
        pltpu.make_async_copy(ref, ref, sem).wait()

    def same_core(d):
        return {"member": 2 * peer(d) + core}

    loads = [
        pltpu.make_async_copy(p_hbm, pv, local_sem.at[0]),
        pltpu.make_async_copy(c_hbm, cv, local_sem.at[1]),
        pltpu.make_async_copy(owner_hbm, owner, local_sem.at[2]),
        pltpu.make_async_copy(map_hbm, mv, local_sem.at[3]),
        pltpu.make_async_copy(ter_hbm, tv, local_sem.at[4]),
    ]
    for load in loads:
        load.start()
    barrier = pltpu.get_barrier_semaphore()

    def greet(device):
        pl.semaphore_signal(barrier, inc=1, device_id=device, device_id_type=MESH)

    corners = [(e, w) for e in range(2) for w in range(2)]
    to_corner = {(e, w): {"dx": x + (1, -1)[w], "dy": y + (1, -1)[e]} for e, w in corners}
    gives_corner = {(e, w): jnp.logical_and((has_e, has_w)[w], (has_n, has_s)[e]) for e, w in corners}
    takes_corner = {(e, w): jnp.logical_and((has_w, has_e)[w], (has_s, has_n)[e]) for e, w in corners}
    second = 2 * chip + 1
    pl.when(core == 1)(lambda: greet(partner))
    odd = lax.rem(x, 2) == 1
    even = jnp.logical_not(odd)
    across = [(has_w, {"dx": x - 1}), (has_e, {"dx": x + 1})] + [(gives_corner[key], to_corner[key]) for key in corners]
    number_across = sum(there.astype(jnp.int32) for there, _ in across)
    for there, device in across:
        pl.when(jnp.logical_and(even, there))(lambda device=device: greet({"member": second, **device}))
    for d in far_first:
        greet({"member": 2 * peer(d) + 1})
    pl.when(has_s)(lambda: greet({"member": second, "dy": y - 1}))
    pl.when(has_n)(lambda: greet({"member": second, "dy": y + 1}))

    level = lax.broadcasted_iota(jnp.int32, TILE, 0)
    lane = lax.broadcasted_iota(jnp.int32, TILE, 1)
    level_f = level.astype(F32)
    zero = jnp.zeros(TILE, F32)

    for load in loads:
        load.wait()
    weight = F32(0.0)
    for rank in range(members):
        value = 2.0 * (members - rank) / (members * (members + 1.0))
        weight = weight + jnp.where(owner[rank] == me, F32(value), F32(0.0))

    def first(r, carry, keep=None):
        for f in range(FIELDS):
            state = pv[pl.ds(f * LEV * ROWS + r, LEV, stride=ROWS), :]
            other = cv[pl.ds(f * LEV * ROWS + r, LEV, stride=ROWS), :]
            s0[r + WIDTH, f] = state
            if keep is not None:
                ph[r - keep, f] = state
            q[r, f] = weight * other - (1.0 / members) * state
        return carry

    lax.fori_loop(0, WIDTH, functools.partial(first, keep=0), 0, unroll=2)
    lax.fori_loop(ROWS - WIDTH, ROWS, functools.partial(first, keep=ROWS - 2 * WIDTH), 0, unroll=2)

    def tell(sem):
        pl.semaphore_signal(sem, inc=1, device_id=partner, device_id_type=MESH)

    def first_core():
        pl.semaphore_wait(barrier, 1)
        tell(hello)

    pl.when(core == 0)(first_core)
    pl.when(core == 1)(lambda: pl.semaphore_wait(hello, 1))

    def dd(kind, d):
        rows = pl.ds(own_b(kind, peer(d)) - WIDTH, part)
        return remote(q.at[rows, theirs], qr.at[rows], out_s, dd_r.at[d] if kind == 0 else dm_r, partner)

    def p_halo(side):
        src, dst, step = ((0, WIDTH + ROWS, -1), (WIDTH, 0, 1))[side]
        return remote(
            ph.at[pl.ds(src, WIDTH)], s0.at[pl.ds(dst, WIDTH), pl.ds(0, FIELDS)],
            ph_s.at[side], ph_r.at[side], {"dx": x + step},
        )

    def mt_halo(side):
        return remote(mts.at[side], mtr.at[side], mt_s.at[side], mt_r.at[side], {"dx": x + (-1, 1)[side]})

    def rs(kind, d):
        return remote(
            t.at[pl.ds(own_b(kind, peer(d)) - WIDTH, part)], rr.at[kind, pl.ds((d - 1) * part, part)],
            out_s, rs_r.at[kind], same_core(d),
        )

    def swap(kind):
        if kind == 1:
            arrived(qr.at[pl.ds(WIDTH, ROWS // 2)], dm_r)
        for d in order:
            if kind == 0:
                dd(kind, d).wait_recv()
            b = own_b(kind, peer(d)) - WIDTH
            for n in range(part):
                for f in range(HALF):
                    t[b + n, f] = q[b + n, HALF * core + f] + qr[b + n, f]

    for d in order:
        dd(0, d).start()
    lax.fori_loop(WIDTH, ROWS - WIDTH, first, 0, unroll=2)
    for d in order:
        dd(1, d).start()
    swap(0)
    swap(1)

    def second_core():
        others = has_s.astype(jnp.int32) + has_n.astype(jnp.int32) + odd.astype(jnp.int32) * number_across
        pl.semaphore_wait(barrier, 2 * (chips - 1) + 2 * others)
        tell(ready)
        for there, device in across:
            def answer(device=device):
                pl.semaphore_signal(far, inc=1, device_id={"member": second, **device}, device_id_type=MESH)

            pl.when(jnp.logical_and(odd, there))(answer)

    pl.when(core == 1)(second_core)
    pl.when(core == 0)(lambda: pl.semaphore_wait(ready, 1))
    for kind in range(2):
        for d in far_first:
            rs(kind, d).start()
    def send_states():
        pl.when(has_w)(lambda: p_halo(0).start())
        pl.when(has_e)(lambda: p_halo(1).start())

    pl.when(odd)(send_states)
    for side, there in ((0, has_w), (1, has_e)):
        sent.append(lambda side=side, there=there: pl.when(there)(p_halo(side).wait_send))

    for side, start in ((0, 0), (1, ROWS - WIDTH)):
        mts[side, pl.ds(0, WIDTH), :] = mv[pl.ds(start, WIDTH), :]
        mts[side, pl.ds(WIDTH, WIDTH), :] = tv[pl.ds(start, WIDTH), :].astype(F32)
    for side, there in ((0, has_w), (1, has_e)):
        sent.append(lambda side=side, there=there: pl.when(there)(mt_halo(side).wait_send))

    quad = lax.div(lane, WIDTH)

    def p_corner(e, w):
        return remote(pcs.at[e, w], pcr.at[e, w], pc_s.at[e, w], pc_r.at[e, w], to_corner[e, w])

    for e, w in corners:
        packed = zero
        for f in range(FIELDS):
            for k in range(WIDTH):
                place = f * 2 * WIDTH + w * WIDTH + k
                row = s0[(ROWS, WIDTH)[w] + k, f]
                packed = jnp.where(quad == place, pltpu.roll(row, (place + 1 - e) * WIDTH % COLS, 1), packed)
        pcs[e, w] = packed
        sent.append(lambda e=e, w=w: pl.when(gives_corner[e, w])(p_corner(e, w).wait_send))

        def no_corner(e=e, w=w):
            pcr[e, w] = zero

        pl.when(jnp.logical_not(takes_corner[e, w]))(no_corner)

    def send_small():
        for side, there in ((0, has_w), (1, has_e)):
            pl.when(there)(lambda side=side: mt_halo(side).start())
        for e, w in corners:
            pl.when(gives_corner[e, w])(lambda e=e, w=w: p_corner(e, w).start())

    pl.when(odd)(send_small)

    def factors(r, carry):
        s0[r + WIDTH, METRIC] = jnp.broadcast_to(mv[pl.ds(r, 1), :] * (-0.5 * integration_step), TILE)
        ground = jnp.broadcast_to(tv[pl.ds(r, 1), :], TILE)
        s0[r + WIDTH, MASK] = (level >= ground).astype(F32)
        return carry

    lax.fori_loop(0, ROWS, factors, 0)

    def empty(b0, side):
        def body():
            for b in range(WIDTH):
                for f in range(FIELDS):
                    s0[b0 + b, f] = zero
                    dx_rows[b0 + b, f] = zero
            mtr[side, pl.ds(0, WIDTH), :] = jnp.ones((WIDTH, COLS), F32)
            mtr[side, pl.ds(WIDTH, WIDTH), :] = jnp.full((WIDTH, COLS), F32(2 * LEV))
            for n in range(chips):
                cs[side * chips + n] = zero
        return body

    pl.when(jnp.logical_not(has_w))(empty(0, 1))
    pl.when(jnp.logical_not(has_e))(empty(WIDTH + ROWS, 0))

    def no_edge(side):
        def body():
            for f in range(FIELDS + 2):
                er[side, f] = zero
            crr[side] = zero
        return body

    pl.when(jnp.logical_not(has_s))(no_edge(0))
    pl.when(jnp.logical_not(has_n))(no_edge(1))

    at = x + 2 * top(chip) - 1
    gives = jnp.logical_and(at >= 0, at < nx)
    takes = came_from(chip)
    halo_here = pl.ds(halo_b(chip), part)
    hx = remote(
        dx_rows.at[pl.ds(own_b(0, chip), part), mine], dx_rows.at[halo_here, mine], hx_s, hx_r, {"dx": at}
    )

    def ag(kind, d):
        rows = pl.ds(own_b(kind, chip), part)
        return remote(
            dx_rows.at[rows, mine], dx_rows.at[rows, mine], out_s, ag_r.at[d - 1], same_core(d)
        )

    def fw(kind, d):
        rows = pl.ds(own_b(kind, source(d)), part)
        return remote(dx_rows.at[rows, mine], dx_rows.at[rows, mine], out_s, fw_r, partner)

    def ha(d):
        return remote(
            dx_rows.at[halo_here, mine], dx_rows.at[halo_here, mine], ha_s, ha_r.at[d - 1], same_core(d)
        )

    def both(d):
        rows = dx_rows.at[halo_here, mine]
        return remote(rows, rows, ha_s, hf_r.at[top(chip)], {"member": 2 * peer(d) + 1 - core})

    def hf(d):
        rows = pl.ds(halo_b(source(d)), part)
        return remote(dx_rows.at[rows, mine], dx_rows.at[rows, mine], hf_s.at[d], hf_r.at[top(source(d))], partner)

    def d_corner(e):
        return remote(dcs.at[e], crr.at[e], dc_s.at[e], dc_r.at[e], {"dx": at, "dy": y + (1, -1)[e]})

    def send_sums():
        hx.start()
        pl.when(has_n)(lambda: d_corner(0).start())
        pl.when(has_s)(lambda: d_corner(1).start())

    def cc(member):
        return remote(crm, cs.at[me], cs_s, cs_r.at[top(chip)], {"member": member})

    own_cc = pltpu.make_async_copy(crm, cs.at[me], cs_r.at[top(chip)])

    for kind in range(2):
        b = own_b(kind, chip)
        total = [[t[b - WIDTH + n, f] for f in range(HALF)] for n in range(part)]
        arrived(rr.at[kind], rs_r.at[kind])
        for d in near_first:
            for n in range(part):
                for f in range(HALF):
                    total[n][f] = total[n][f] + rr[kind, (d - 1) * part + n, f]
        for n in range(part):
            for f in range(HALF):
                dx_rows[b + n, HALF * core + f] = total[n][f]
        if kind == 0:
            north, south = zero, zero
            for n in range(part):
                for f in range(HALF):
                    place = (HALF * core + f) * 2 * WIDTH + chip * part + n + WIDTH - 2 * WIDTH * top(chip)
                    other = lax.rem(place + 16, 32)
                    north = jnp.where(quad == place, pltpu.roll(total[n][f], lax.rem(place + 1, 32) * WIDTH, 1), north)
                    south = jnp.where(quad == other, pltpu.roll(total[n][f], other * WIDTH, 1), south)
            dcs[0] = north
            dcs[1] = south
            pl.when(jnp.logical_and(odd, gives))(send_sums)
            for e, there in ((0, has_n), (1, has_s)):
                going = jnp.logical_and(gives, there)
                sent.append(lambda e=e, going=going: pl.when(going)(d_corner(e).wait_send))
            sent.append(lambda: pl.when(gives)(hx.wait_send))
        for d in far_first:
            ag(kind, d).start()
        fw(kind, 0).start()

    inner = lax.rem(lane, 16)
    block = lax.div(lane, 16)

    def pack_rows(rows, old):
        def body(f, carry):
            for i in range(STRIP):
                groups = [g for g in range(GROUPS) if g * STRIP + i in rows]
                if not groups:
                    continue
                packed = a0[i + 1, f] if old else zero
                for g in groups:
                    row = s0[g * STRIP + i, f]
                    left = jnp.logical_and(block == g, inner >= WIDTH)
                    right = jnp.logical_and(block == GROUPS + g, inner < 16 - WIDTH)
                    packed = jnp.where(left, pltpu.roll(row, 16 * g + WIDTH, 1), packed)
                    packed = jnp.where(right, pltpu.roll(row, 16 * g + 76, 1), packed)
                a0[i + 1, f] = packed
            return carry
        return body

    inside = range(WIDTH, WIDTH + ROWS)
    outside = [b for b in range(TALL) if b not in inside]

    def edge(side, late):
        fields = pl.ds(0, FIELDS) if late else pl.ds(FIELDS, 2)
        k = side + 2 * late
        return remote(es.at[side, fields], er.at[side, fields], ed_s.at[k], ed_r.at[k], {"dy": y + (1, -1)[side]})

    def send_edges(late):
        for f in range(FIELDS) if late else (METRIC, MASK):
            north, south = zero, zero
            for i in range(STRIP):
                strip = a0[i + 1, f]
                at_lane = (i // 4) * 64 + (i % 4) * 4
                slot = jnp.logical_and(lax.div(lane, 64) == i // 4, lax.div(inner, 4) == i % 4)
                north = jnp.where(slot, pltpu.roll(strip, (at_lane - 72) % COLS, 1), north)
                south = jnp.where(slot, pltpu.roll(strip, (at_lane - 4) % COLS, 1), south)
            es[0, f] = north
            es[1, f] = south
        for side, there in ((0, has_n), (1, has_s)):
            pl.when(there)(lambda side=side: edge(side, late).start())
            sent.append(lambda side=side, there=there: pl.when(there)(edge(side, late).wait_send))

    def gather(ds):
        for d in ds:
            arrived(dx_rows.at[pl.ds(0, 2 * part), mine], ag_r.at[d - 1])
            for kind in range(2):
                fw(kind, d).start()

    starts_last = jnp.logical_and(x == 0, y == 0)
    pl.when(jnp.logical_not(starts_last))(lambda: gather(near_first))

    def all_answered():
        pl.semaphore_wait(far, number_across)
        tell(ready_far)

    pl.when(jnp.logical_and(even, core == 1))(all_answered)
    pl.when(jnp.logical_and(even, core == 0))(lambda: pl.semaphore_wait(ready_far, 1))

    def send_across():
        pl.when(gives)(send_sums)
        send_states()
        send_small()

    pl.when(even)(send_across)

    def halo_factors(side, b0):
        for b in range(WIDTH):
            s0[b0 + b, METRIC] = jnp.broadcast_to(mtr[side, pl.ds(b, 1), :] * (-0.5 * integration_step), TILE)
            ground = jnp.broadcast_to(mtr[side, pl.ds(WIDTH + b, 1), :], TILE)
            s0[b0 + b, MASK] = (level_f >= ground).astype(F32)

    pl.when(has_e)(lambda: mt_halo(0).wait_recv())
    pl.when(has_w)(lambda: mt_halo(1).wait_recv())
    halo_factors(0, WIDTH + ROWS)
    halo_factors(1, 0)
    lax.fori_loop(FIELDS, FIELDS + 2, pack_rows(range(TALL), False), 0, unroll=True)

    send_edges(0)

    def spread_halo():
        hx.wait_recv()
        for d in far_first:
            ha(d).start()
            if d in direct:
                both(d).start()
        hf(0).start()

    pl.when(takes)(spread_halo)

    spread_bytes = q.at[pl.ds(0, (chips - 1 + len(direct)) * part * HALF // FIELDS)]
    sent.append(lambda: pl.when(takes)(lambda: arrived(spread_bytes, ha_s)))
    def spread_corner():
        for e, there in ((0, has_s), (1, has_n)):
            pl.when(there)(lambda e=e: d_corner(e).wait_recv())
        crm[...] = crr[0] + crr[1]
        own_cc.start()
        for d in far_first:
            for co in range(2):
                cc(2 * peer(d) + co).start()
        cc(me + 1 - 2 * core).start()

    pl.when(takes)(spread_corner)
    sent.append(lambda: pl.when(takes)(lambda: arrived(cs.at[pl.ds(0, members - 1)], cs_s)))
    pl.when(starts_last)(lambda: gather(near_first))
    arrived(dx_rows.at[pl.ds(0, ROWS), mine], fw_r)


    def begin(b, carry):
        for f in range(FIELDS):
            s0[b, f] = s0[b, f] + dx_rows[b, f]
        return carry

    lax.fori_loop(WIDTH, WIDTH + ROWS, begin, 0, unroll=True)
    lax.fori_loop(0, FIELDS, pack_rows(inside, False), 0, unroll=True)
    send_edges(1)
    states = (s0, s1, s2, s3, s4)
    for step in range(1, STEPS + 1):
        def row(b, carry, src=states[step - 1], dst=states[step]):
            stencil(src, dst, b, s0[b, METRIC], s0[b, MASK], level)
            return carry

        lax.fori_loop(WIDTH + step, WIDTH + ROWS - step, row, 0, unroll=True)

    for d in near_first:
        def pass_on(d=d):
            ha(d).wait_recv()
            if d not in direct:
                hf(d).start()

        pl.when(came_from(source(d)))(pass_on)
    for late in range(2):
        pl.when(has_s)(lambda late=late: edge(0, late).wait_recv())
        pl.when(has_n)(lambda late=late: edge(1, late).wait_recv())
    for i in range(STRIP):
        at_lane = (i // 4) * 64 + (i % 4) * 4
        left = jnp.logical_and(block < GROUPS, inner < WIDTH)
        right = jnp.logical_and(block >= GROUPS, inner >= 16 - WIDTH)
        for f in range(FIELDS + 2):
            strip = a0[i + 1, f]
            strip = jnp.where(left, pltpu.roll(er[0, f], (-at_lane) % COLS, 1), strip)
            strip = jnp.where(right, pltpu.roll(er[1, f], (76 - at_lane) % COLS, 1), strip)
            a0[i + 1, f] = strip
    for d in range(chips):
        if d not in direct:
            sent.append(lambda d=d: pl.when(came_from(source(d)))(hf(d).wait_send))
    for side, there in ((0, has_e), (1, has_w)):
        rows = dx_rows.at[pl.ds(0, WIDTH), mine]
        pl.when(there)(lambda side=side, rows=rows: arrived(rows, hf_r.at[side]))
    pl.when(has_e)(lambda: p_halo(0).wait_recv())
    pl.when(has_w)(lambda: p_halo(1).wait_recv())
    lax.fori_loop(0, WIDTH, begin, 0, unroll=True)
    lax.fori_loop(WIDTH + ROWS, TALL, begin, 0, unroll=True)

    lax.fori_loop(0, FIELDS, pack_rows(outside, True), 0, unroll=True)

    for step in range(1, STEPS + 1):
        def rows(j, carry, src=states[step - 1], dst=states[step], step=step):
            for b in (step + j, WIDTH + ROWS - step + j):
                stencil(src, dst, b, s0[b, METRIC], s0[b, MASK], level)
            return carry

        lax.fori_loop(0, WIDTH, rows, 0, unroll=True)

    for e, w in corners:
        pl.when(takes_corner[e, w])(lambda e=e, w=w: p_corner(e, w).wait_recv())
    for side, there in ((0, has_e), (1, has_w)):
        pl.when(there)(lambda side=side: arrived(cs.at[pl.ds(side * chips, chips)], cs_r.at[side]))
    by_core = [functools.reduce(jnp.add, [cs[2 * ch + co] for ch in range(chips)]) for co in range(2)]
    low = lane < COLS // 2
    from_south = jnp.where(low, by_core[0], by_core[1]) + (pcr[0, 0] + pcr[0, 1])
    from_north = pltpu.roll(jnp.where(low, by_core[1], by_core[0]), COLS // 2, 1) + (pcr[1, 0] + pcr[1, 1])
    for n, b in enumerate(outside):
        g, i = divmod(b, STRIP)
        left = jnp.logical_and(block == g, inner < WIDTH)
        right = jnp.logical_and(block == GROUPS + g, inner >= 16 - WIDTH)
        for f in range(FIELDS):
            at_lane = f * 32 + n * WIDTH
            strip = a0[i + 1, f]
            strip = jnp.where(left, pltpu.roll(from_south, (16 * g - at_lane) % COLS, 1), strip)
            strip = jnp.where(right, pltpu.roll(from_north, (76 + 16 * g - at_lane) % COLS, 1), strip)
            a0[i + 1, f] = strip
    for step in range(STEPS):
        src, dst = (a0, a1) if step % 2 == 0 else (a1, a0)
        for f in range(FIELDS):
            src[0, f] = pltpu.roll(src[STRIP, f], 16, 1)
            src[STRIP + 1, f] = pltpu.roll(src[1, f], COLS - 16, 1)

        def strip_row(i, carry, src=src, dst=dst):
            stencil(src, dst, i, a0[i, METRIC], a0[i, MASK], level)
            return carry

        lax.fori_loop(1, STRIP + 1, strip_row, 0, unroll=True)

    for g in range(GROUPS):
        def merge(i, carry, g=g):
            for f in range(FIELDS):
                strip = a0[i + 1, f]
                new = s4[g * STRIP + i, f]
                new = jnp.where(lane < WIDTH, pltpu.roll(strip, (-16 * g - WIDTH) % COLS, 1), new)
                new = jnp.where(lane >= COLS - WIDTH, pltpu.roll(strip, (52 - 16 * g) % COLS, 1), new)
                out[pl.ds(f * LEV * ROWS + g * STRIP + i - WIDTH, LEV, stride=ROWS), :] = new
            return carry

        lax.fori_loop(max(0, WIDTH - g * STRIP), min(STRIP, WIDTH + ROWS - g * STRIP), merge, 0, unroll=True)
    arrived(s0.at[pl.ds(0, pieces * part * HALF // (FIELDS + 2))], out_s)
    for wait in sent:
        wait()


def solution(mesh):
    members, nx, ny = (mesh.shape[axis] for axis in ("member", "dx", "dy"))
    chips = members // 2
    part = (ROWS // 2) // chips
    flat = FIELDS * LEV * ROWS

    def on_device(states, control, owner, map_factor, terrain):
        any_space = pl.BlockSpec(memory_space=pl.ANY)
        dma = pltpu.SemaphoreType.DMA
        out = pl.pallas_call(
            functools.partial(kernel, members, nx, ny),
            out_shape=pltpu.VMEM((flat, COLS), F32),
            in_specs=[any_space] * 5,
            out_specs=pl.BlockSpec(memory_space=pltpu.VMEM),
            scratch_shapes=[
                pltpu.VMEM((flat, COLS), F32),
                pltpu.VMEM((flat, COLS), F32),
                pltpu.SMEM((members,), jnp.int32),
                pltpu.VMEM((ROWS, COLS), F32),
                pltpu.VMEM((ROWS, COLS), jnp.int32),
                pltpu.VMEM((TALL, FIELDS + 2) + TILE, F32),
                pltpu.VMEM((TALL, FIELDS) + TILE, F32),
                pltpu.VMEM((TALL, FIELDS) + TILE, F32),
                pltpu.VMEM((TALL, FIELDS) + TILE, F32),
                pltpu.VMEM((TALL, FIELDS) + TILE, F32),
                pltpu.VMEM((ROWS, FIELDS) + TILE, F32),
                pltpu.VMEM((ROWS, HALF) + TILE, F32),
                pltpu.VMEM((ROWS, HALF) + TILE, F32),
                pltpu.VMEM((2, part * (chips - 1), HALF) + TILE, F32),
                pltpu.VMEM((TALL, FIELDS) + TILE, F32),
                pltpu.VMEM((2,) + TILE, F32),
                pltpu.VMEM((2,) + TILE, F32),
                pltpu.VMEM((STRIP + 2, FIELDS + 2) + TILE, F32),
                pltpu.VMEM((STRIP + 2, FIELDS) + TILE, F32),
                pltpu.VMEM((2, FIELDS + 2) + TILE, F32),
                pltpu.VMEM((2, FIELDS + 2) + TILE, F32),
                pltpu.VMEM((2, 2) + TILE, F32),
                pltpu.VMEM((2, 2) + TILE, F32),
                pltpu.VMEM((2,) + TILE, F32),
                pltpu.VMEM((2,) + TILE, F32),
                pltpu.VMEM(TILE, F32),
                pltpu.VMEM((members,) + TILE, F32),
                pltpu.VMEM((2 * WIDTH, FIELDS) + TILE, F32),
                dma((5,)),
                dma, dma((chips,)), dma, dma((2,)), dma((chips - 1,)), dma,
                dma, dma,
                dma, dma((chips - 1,)),
                dma((chips,)), dma((2,)),
                dma((2,)), dma((2,)),
                dma((2,)), dma((2,)),
                dma((4,)), dma((4,)),
                dma((2, 2)), dma((2, 2)),
                dma((2,)), dma((2,)),
                dma, dma((2,)),
                *[pltpu.SemaphoreType.REGULAR] * 4,
            ],
            compiler_params=pltpu.CompilerParams(collective_id=0, has_side_effects=True),
        )(states.reshape(flat, COLS), control.reshape(flat, COLS), owner, map_factor, terrain)
        return out.reshape(states.shape)

    spread = P("member", None, None, "dx", "dy")
    return jax.shard_map(
        on_device,
        mesh=mesh,
        in_specs=(spread, spread, P(), P("dx", "dy"), P("dx", "dy")),
        out_specs=spread,
        check_vma=False,
    )
```

```python
import functools

import jax
import jax.numpy as jnp
from jax import lax
from jax.experimental import pallas as pl
from jax.experimental.pallas import tpu as pltpu
from jax.sharding import PartitionSpec as P

MESH = pl.DeviceIdType.MESH
F32 = jnp.float32

STEPS = 4
FIELDS = 4
HALF = FIELDS // 2
LEV = 8
ROWS = 16
COLS = 128
WIDTH = STEPS
TALL = ROWS + 2 * WIDTH
GROUPS = 4
STRIP = TALL // GROUPS
METRIC, MASK = FIELDS, FIELDS + 1
TILE = (LEV, COLS)

integration_step = 0.2
diffusion = 0.1


def stencil(src, dst, b, metric, mask, level):
    mid = [src[b, f] for f in range(FIELDS)]
    east = [src[b + 1, f] for f in range(FIELDS)]
    west = [src[b - 1, f] for f in range(FIELDS)]
    along_x = metric * mid[0]
    along_y = metric * mid[1]
    new, gx, gy = [], [], []
    for f in range(FIELDS):
        north = pltpu.roll(mid[f], COLS - 1, 1)
        south = pltpu.roll(mid[f], 1, 1)
        above = jnp.where(level < LEV - 1, pltpu.roll(mid[f], LEV - 1, 0), 0.0)
        below = jnp.where(level > 0, pltpu.roll(mid[f], 1, 0), 0.0)
        gx.append(east[f] - west[f])
        gy.append(north - south)
        six = (east[f] + west[f]) + (north + south) + (above + below)
        flow = along_x * gx[f] + along_y * gy[f]
        rate = integration_step * diffusion
        new.append((1.0 - 6.0 * rate) * mid[f] + rate * six + flow)
    new[0] = new[0] + metric * gx[2]
    new[1] = new[1] + metric * gy[2]
    new[2] = new[2] + metric * (gx[0] + gy[1])
    for f in range(FIELDS):
        dst[b, f] = mask * new[f]


def kernel(
    members, nx, ny,
    p_hbm, c_hbm, owner_hbm, map_hbm, ter_hbm, out,
    pv, cv, owner, mv, tv, s0, s1, s2, s3, s4, q, qr, t, rr, dx_rows, mts, mtr, a0, a1, es, er, pcs, pcr, dcs, crr, crm, cs, ph,
    local_sem, out_s, dd_r, dm_r, rs_r, ag_r, fw_r, hx_s, hx_r, ha_s, ha_r, hf_s, hf_r,
    ph_s, ph_r, mt_s, mt_r, ed_s, ed_r, pc_s, pc_r, dc_s, dc_r, cs_s, cs_r, hello, ready, far, ready_far,
):
    chips = members // 2
    part = (ROWS // 2) // chips
    me = lax.axis_index("member")
    x = lax.axis_index("dx")
    y = lax.axis_index("dy")
    chip = lax.div(me, 2)
    core = lax.rem(me, 2)
    partner = {"member": me + 1 - 2 * core}
    has_w, has_e = x > 0, x < nx - 1
    has_s, has_n = y > 0, y < ny - 1
    far_first = sorted(range(1, chips), key=lambda d: -min(d, chips - d))
    near_first = far_first[::-1]
    order = far_first + [0]
    direct = [d for d in far_first if min(d, chips - d) > 3]
    mine = pl.ds(HALF * core, HALF)
    theirs = pl.ds(HALF * (1 - core), HALF)
    sent = []
    pieces = 2 * chips + 2 * (chips - 1) + 2 * (chips - 1) + 2 * chips

    def peer(d):
        return lax.rem(chip + d, chips)

    def source(d):
        return lax.rem(chip + chips - d, chips)

    def top(ch):
        return lax.div(2 * ch, chips)

    def own_b(kind, ch):
        if kind == 0:
            return WIDTH + ch * part + (ROWS // 2) * top(ch)
        return 2 * WIDTH + ch * part

    def halo_b(ch):
        return ch * part + (WIDTH + ROWS) - TALL * top(ch)

    def came_from(ch):
        at = x + 1 - 2 * top(ch)
        return jnp.logical_and(at >= 0, at < nx)

    def remote(src, dst, ss, rs, device):
        return pltpu.make_async_remote_copy(
            src_ref=src, dst_ref=dst, send_sem=ss, recv_sem=rs, device_id=device, device_id_type=MESH
        )

    def arrived(ref, sem):
        pltpu.make_async_copy(ref, ref, sem).wait()

    def same_core(d):
        return {"member": 2 * peer(d) + core}

    loads = [
        pltpu.make_async_copy(p_hbm, pv, local_sem.at[0]),
        pltpu.make_async_copy(c_hbm, cv, local_sem.at[1]),
        pltpu.make_async_copy(owner_hbm, owner, local_sem.at[2]),
        pltpu.make_async_copy(map_hbm, mv, local_sem.at[3]),
        pltpu.make_async_copy(ter_hbm, tv, local_sem.at[4]),
    ]
    for load in loads:
        load.start()
    barrier = pltpu.get_barrier_semaphore()

    def greet(device):
        pl.semaphore_signal(barrier, inc=1, device_id=device, device_id_type=MESH)

    corners = [(e, w) for e in range(2) for w in range(2)]
    to_corner = {(e, w): {"dx": x + (1, -1)[w], "dy": y + (1, -1)[e]} for e, w in corners}
    gives_corner = {(e, w): jnp.logical_and((has_e, has_w)[w], (has_n, has_s)[e]) for e, w in corners}
    takes_corner = {(e, w): jnp.logical_and((has_w, has_e)[w], (has_s, has_n)[e]) for e, w in corners}
    second = 2 * chip + 1
    pl.when(core == 1)(lambda: greet(partner))
    odd = lax.rem(x, 2) == 1
    even = jnp.logical_not(odd)
    across = [(has_w, {"dx": x - 1}), (has_e, {"dx": x + 1})] + [(gives_corner[key], to_corner[key]) for key in corners]
    number_across = sum(there.astype(jnp.int32) for there, _ in across)
    for there, device in across:
        pl.when(jnp.logical_and(even, there))(lambda device=device: greet({"member": second, **device}))
    for d in far_first:
        greet({"member": 2 * peer(d) + 1})
    pl.when(has_s)(lambda: greet({"member": second, "dy": y - 1}))
    pl.when(has_n)(lambda: greet({"member": second, "dy": y + 1}))

    level = lax.broadcasted_iota(jnp.int32, TILE, 0)
    lane = lax.broadcasted_iota(jnp.int32, TILE, 1)
    level_f = level.astype(F32)
    zero = jnp.zeros(TILE, F32)

    for load in loads:
        load.wait()
    weight = F32(0.0)
    for rank in range(members):
        value = 2.0 * (members - rank) / (members * (members + 1.0))
        weight = weight + jnp.where(owner[rank] == me, F32(value), F32(0.0))

    def first(r, carry, keep=None):
        for f in range(FIELDS):
            state = pv[pl.ds(f * LEV * ROWS + r, LEV, stride=ROWS), :]
            other = cv[pl.ds(f * LEV * ROWS + r, LEV, stride=ROWS), :]
            s0[r + WIDTH, f] = state
            if keep is not None:
                ph[r - keep, f] = state
            q[r, f] = weight * other - (1.0 / members) * state
        return carry

    lax.fori_loop(0, WIDTH, functools.partial(first, keep=0), 0, unroll=2)
    lax.fori_loop(ROWS - WIDTH, ROWS, functools.partial(first, keep=ROWS - 2 * WIDTH), 0, unroll=2)

    def tell(sem):
        pl.semaphore_signal(sem, inc=1, device_id=partner, device_id_type=MESH)

    def first_core():
        pl.semaphore_wait(barrier, 1)
        tell(hello)

    pl.when(core == 0)(first_core)
    pl.when(core == 1)(lambda: pl.semaphore_wait(hello, 1))

    def dd(kind, d):
        rows = pl.ds(own_b(kind, peer(d)) - WIDTH, part)
        return remote(q.at[rows, theirs], qr.at[rows], out_s, dd_r.at[d] if kind == 0 else dm_r, partner)

    def p_halo(side):
        src, dst, step = ((0, WIDTH + ROWS, -1), (WIDTH, 0, 1))[side]
        return remote(
            ph.at[pl.ds(src, WIDTH)], s0.at[pl.ds(dst, WIDTH), pl.ds(0, FIELDS)],
            ph_s.at[side], ph_r.at[side], {"dx": x + step},
        )

    def mt_halo(side):
        return remote(mts.at[side], mtr.at[side], mt_s.at[side], mt_r.at[side], {"dx": x + (-1, 1)[side]})

    def rs(kind, d):
        return remote(
            t.at[pl.ds(own_b(kind, peer(d)) - WIDTH, part)], rr.at[kind, pl.ds((d - 1) * part, part)],
            out_s, rs_r.at[kind], same_core(d),
        )

    def swap(kind):
        if kind == 1:
            arrived(qr.at[pl.ds(WIDTH, ROWS // 2)], dm_r)
        for d in order:
            if kind == 0:
                dd(kind, d).wait_recv()
            b = own_b(kind, peer(d)) - WIDTH
            for n in range(part):
                for f in range(HALF):
                    t[b + n, f] = q[b + n, HALF * core + f] + qr[b + n, f]

    for d in order:
        dd(0, d).start()
    lax.fori_loop(WIDTH, ROWS - WIDTH, first, 0, unroll=2)
    for d in order:
        dd(1, d).start()
    swap(0)
    swap(1)

    def second_core():
        others = has_s.astype(jnp.int32) + has_n.astype(jnp.int32) + odd.astype(jnp.int32) * number_across
        pl.semaphore_wait(barrier, 2 * (chips - 1) + 2 * others)
        tell(ready)
        for there, device in across:
            def answer(device=device):
                pl.semaphore_signal(far, inc=1, device_id={"member": second, **device}, device_id_type=MESH)

            pl.when(jnp.logical_and(odd, there))(answer)

    pl.when(core == 1)(second_core)
    pl.when(core == 0)(lambda: pl.semaphore_wait(ready, 1))
    for kind in range(2):
        for d in far_first:
            rs(kind, d).start()
    def send_states():
        pl.when(has_w)(lambda: p_halo(0).start())
        pl.when(has_e)(lambda: p_halo(1).start())

    pl.when(odd)(send_states)
    for side, there in ((0, has_w), (1, has_e)):
        sent.append(lambda side=side, there=there: pl.when(there)(p_halo(side).wait_send))

    for side, start in ((0, 0), (1, ROWS - WIDTH)):
        mts[side, pl.ds(0, WIDTH), :] = mv[pl.ds(start, WIDTH), :]
        mts[side, pl.ds(WIDTH, WIDTH), :] = tv[pl.ds(start, WIDTH), :].astype(F32)
    for side, there in ((0, has_w), (1, has_e)):
        sent.append(lambda side=side, there=there: pl.when(there)(mt_halo(side).wait_send))

    quad = lax.div(lane, WIDTH)

    def p_corner(e, w):
        return remote(pcs.at[e, w], pcr.at[e, w], pc_s.at[e, w], pc_r.at[e, w], to_corner[e, w])

    for e, w in corners:
        packed = zero
        for f in range(FIELDS):
            for k in range(WIDTH):
                place = f * 2 * WIDTH + w * WIDTH + k
                row = s0[(ROWS, WIDTH)[w] + k, f]
                packed = jnp.where(quad == place, pltpu.roll(row, (place + 1 - e) * WIDTH % COLS, 1), packed)
        pcs[e, w] = packed
        sent.append(lambda e=e, w=w: pl.when(gives_corner[e, w])(p_corner(e, w).wait_send))

        def no_corner(e=e, w=w):
            pcr[e, w] = zero

        pl.when(jnp.logical_not(takes_corner[e, w]))(no_corner)

    def send_small():
        for side, there in ((0, has_w), (1, has_e)):
            pl.when(there)(lambda side=side: mt_halo(side).start())
        for e, w in corners:
            pl.when(gives_corner[e, w])(lambda e=e, w=w: p_corner(e, w).start())

    pl.when(odd)(send_small)

    def factors(r, carry):
        s0[r + WIDTH, METRIC] = jnp.broadcast_to(mv[pl.ds(r, 1), :] * (-0.5 * integration_step), TILE)
        ground = jnp.broadcast_to(tv[pl.ds(r, 1), :], TILE)
        s0[r + WIDTH, MASK] = (level >= ground).astype(F32)
        return carry

    lax.fori_loop(0, ROWS, factors, 0)

    def empty(b0, side):
        def body():
            for b in range(WIDTH):
                for f in range(FIELDS):
                    s0[b0 + b, f] = zero
                    dx_rows[b0 + b, f] = zero
            mtr[side, pl.ds(0, WIDTH), :] = jnp.ones((WIDTH, COLS), F32)
            mtr[side, pl.ds(WIDTH, WIDTH), :] = jnp.full((WIDTH, COLS), F32(2 * LEV))
            for n in range(chips):
                cs[side * chips + n] = zero
        return body

    pl.when(jnp.logical_not(has_w))(empty(0, 1))
    pl.when(jnp.logical_not(has_e))(empty(WIDTH + ROWS, 0))

    def no_edge(side):
        def body():
            for f in range(FIELDS + 2):
                er[side, f] = zero
            crr[side] = zero
        return body

    pl.when(jnp.logical_not(has_s))(no_edge(0))
    pl.when(jnp.logical_not(has_n))(no_edge(1))

    at = x + 2 * top(chip) - 1
    gives = jnp.logical_and(at >= 0, at < nx)
    takes = came_from(chip)
    halo_here = pl.ds(halo_b(chip), part)
    hx = remote(
        dx_rows.at[pl.ds(own_b(0, chip), part), mine], dx_rows.at[halo_here, mine], hx_s, hx_r, {"dx": at}
    )

    def ag(kind, d):
        rows = pl.ds(own_b(kind, chip), part)
        return remote(
            dx_rows.at[rows, mine], dx_rows.at[rows, mine], out_s, ag_r.at[d - 1], same_core(d)
        )

    def fw(kind, d):
        rows = pl.ds(own_b(kind, source(d)), part)
        return remote(dx_rows.at[rows, mine], dx_rows.at[rows, mine], out_s, fw_r, partner)

    def ha(d):
        return remote(
            dx_rows.at[halo_here, mine], dx_rows.at[halo_here, mine], ha_s, ha_r.at[d - 1], same_core(d)
        )

    def both(d):
        rows = dx_rows.at[halo_here, mine]
        return remote(rows, rows, ha_s, hf_r.at[top(chip)], {"member": 2 * peer(d) + 1 - core})

    def hf(d):
        rows = pl.ds(halo_b(source(d)), part)
        return remote(dx_rows.at[rows, mine], dx_rows.at[rows, mine], hf_s.at[d], hf_r.at[top(source(d))], partner)

    def d_corner(e):
        return remote(dcs.at[e], crr.at[e], dc_s.at[e], dc_r.at[e], {"dx": at, "dy": y + (1, -1)[e]})

    def send_sums():
        hx.start()
        pl.when(has_n)(lambda: d_corner(0).start())
        pl.when(has_s)(lambda: d_corner(1).start())

    def cc(member):
        return remote(crm, cs.at[me], cs_s, cs_r.at[top(chip)], {"member": member})

    own_cc = pltpu.make_async_copy(crm, cs.at[me], cs_r.at[top(chip)])

    for kind in range(2):
        b = own_b(kind, chip)
        total = [[t[b - WIDTH + n, f] for f in range(HALF)] for n in range(part)]
        arrived(rr.at[kind], rs_r.at[kind])
        for d in near_first:
            for n in range(part):
                for f in range(HALF):
                    total[n][f] = total[n][f] + rr[kind, (d - 1) * part + n, f]
        for n in range(part):
            for f in range(HALF):
                dx_rows[b + n, HALF * core + f] = total[n][f]
        if kind == 0:
            north, south = zero, zero
            for n in range(part):
                for f in range(HALF):
                    place = (HALF * core + f) * 2 * WIDTH + chip * part + n + WIDTH - 2 * WIDTH * top(chip)
                    other = lax.rem(place + 16, 32)
                    north = jnp.where(quad == place, pltpu.roll(total[n][f], lax.rem(place + 1, 32) * WIDTH, 1), north)
                    south = jnp.where(quad == other, pltpu.roll(total[n][f], other * WIDTH, 1), south)
            dcs[0] = north
            dcs[1] = south
            pl.when(jnp.logical_and(odd, gives))(send_sums)
            for e, there in ((0, has_n), (1, has_s)):
                going = jnp.logical_and(gives, there)
                sent.append(lambda e=e, going=going: pl.when(going)(d_corner(e).wait_send))
            sent.append(lambda: pl.when(gives)(hx.wait_send))
        for d in far_first:
            ag(kind, d).start()
        fw(kind, 0).start()

    inner = lax.rem(lane, 16)
    block = lax.div(lane, 16)

    def pack_rows(rows, old):
        def body(f, carry):
            for i in range(STRIP):
                groups = [g for g in range(GROUPS) if g * STRIP + i in rows]
                if not groups:
                    continue
                packed = a0[i + 1, f] if old else zero
                for g in groups:
                    row = s0[g * STRIP + i, f]
                    left = jnp.logical_and(block == g, inner >= WIDTH)
                    right = jnp.logical_and(block == GROUPS + g, inner < 16 - WIDTH)
                    packed = jnp.where(left, pltpu.roll(row, 16 * g + WIDTH, 1), packed)
                    packed = jnp.where(right, pltpu.roll(row, 16 * g + 76, 1), packed)
                a0[i + 1, f] = packed
            return carry
        return body

    inside = range(WIDTH, WIDTH + ROWS)
    outside = [b for b in range(TALL) if b not in inside]

    def edge(side, late):
        fields = pl.ds(0, FIELDS) if late else pl.ds(FIELDS, 2)
        k = side + 2 * late
        return remote(es.at[side, fields], er.at[side, fields], ed_s.at[k], ed_r.at[k], {"dy": y + (1, -1)[side]})

    def send_edges(late):
        for f in range(FIELDS) if late else (METRIC, MASK):
            north, south = zero, zero
            for i in range(STRIP):
                strip = a0[i + 1, f]
                at_lane = (i // 4) * 64 + (i % 4) * 4
                slot = jnp.logical_and(lax.div(lane, 64) == i // 4, lax.div(inner, 4) == i % 4)
                north = jnp.where(slot, pltpu.roll(strip, (at_lane - 72) % COLS, 1), north)
                south = jnp.where(slot, pltpu.roll(strip, (at_lane - 4) % COLS, 1), south)
            es[0, f] = north
            es[1, f] = south
        for side, there in ((0, has_n), (1, has_s)):
            pl.when(there)(lambda side=side: edge(side, late).start())
            sent.append(lambda side=side, there=there: pl.when(there)(edge(side, late).wait_send))

    def gather(ds):
        for d in ds:
            arrived(dx_rows.at[pl.ds(0, 2 * part), mine], ag_r.at[d - 1])
            for kind in range(2):
                fw(kind, d).start()

    starts_last = jnp.logical_and(x == 0, y == 0)
    pl.when(jnp.logical_not(starts_last))(lambda: gather(near_first))

    def all_answered():
        pl.semaphore_wait(far, number_across)
        tell(ready_far)

    pl.when(jnp.logical_and(even, core == 1))(all_answered)
    pl.when(jnp.logical_and(even, core == 0))(lambda: pl.semaphore_wait(ready_far, 1))

    def send_across():
        pl.when(gives)(send_sums)
        send_states()
        send_small()

    pl.when(even)(send_across)

    def halo_factors(side, b0):
        for b in range(WIDTH):
            s0[b0 + b, METRIC] = jnp.broadcast_to(mtr[side, pl.ds(b, 1), :] * (-0.5 * integration_step), TILE)
            ground = jnp.broadcast_to(mtr[side, pl.ds(WIDTH + b, 1), :], TILE)
            s0[b0 + b, MASK] = (level_f >= ground).astype(F32)

    pl.when(has_e)(lambda: mt_halo(0).wait_recv())
    pl.when(has_w)(lambda: mt_halo(1).wait_recv())
    halo_factors(0, WIDTH + ROWS)
    halo_factors(1, 0)
    lax.fori_loop(FIELDS, FIELDS + 2, pack_rows(range(TALL), False), 0, unroll=True)

    send_edges(0)

    def spread_halo():
        hx.wait_recv()
        for d in far_first:
            ha(d).start()
            if d in direct:
                both(d).start()
        hf(0).start()

    pl.when(takes)(spread_halo)

    spread_bytes = q.at[pl.ds(0, (chips - 1 + len(direct)) * part * HALF // FIELDS)]
    sent.append(lambda: pl.when(takes)(lambda: arrived(spread_bytes, ha_s)))
    def spread_corner():
        for e, there in ((0, has_s), (1, has_n)):
            pl.when(there)(lambda e=e: d_corner(e).wait_recv())
        crm[...] = crr[0] + crr[1]
        own_cc.start()
        for d in far_first:
            for co in range(2):
                cc(2 * peer(d) + co).start()
        cc(me + 1 - 2 * core).start()

    pl.when(takes)(spread_corner)
    sent.append(lambda: pl.when(takes)(lambda: arrived(cs.at[pl.ds(0, members - 1)], cs_s)))
    pl.when(starts_last)(lambda: gather(near_first))
    arrived(dx_rows.at[pl.ds(0, ROWS), mine], fw_r)


    def begin(b, carry):
        for f in range(FIELDS):
            s0[b, f] = s0[b, f] + dx_rows[b, f]
        return carry

    lax.fori_loop(WIDTH, WIDTH + ROWS, begin, 0, unroll=True)
    lax.fori_loop(0, FIELDS, pack_rows(inside, False), 0, unroll=True)
    send_edges(1)
    states = (s0, s1, s2, s3, s4)
    for step in range(1, STEPS + 1):
        def row(b, carry, src=states[step - 1], dst=states[step]):
            stencil(src, dst, b, s0[b, METRIC], s0[b, MASK], level)
            return carry

        lax.fori_loop(WIDTH + step, WIDTH + ROWS - step, row, 0, unroll=True)

    for d in near_first:
        def pass_on(d=d):
            ha(d).wait_recv()
            if d not in direct:
                hf(d).start()

        pl.when(came_from(source(d)))(pass_on)
    for late in range(2):
        pl.when(has_s)(lambda late=late: edge(0, late).wait_recv())
        pl.when(has_n)(lambda late=late: edge(1, late).wait_recv())
    for i in range(STRIP):
        at_lane = (i // 4) * 64 + (i % 4) * 4
        left = jnp.logical_and(block < GROUPS, inner < WIDTH)
        right = jnp.logical_and(block >= GROUPS, inner >= 16 - WIDTH)
        for f in range(FIELDS + 2):
            strip = a0[i + 1, f]
            strip = jnp.where(left, pltpu.roll(er[0, f], (-at_lane) % COLS, 1), strip)
            strip = jnp.where(right, pltpu.roll(er[1, f], (76 - at_lane) % COLS, 1), strip)
            a0[i + 1, f] = strip
    for d in range(chips):
        if d not in direct:
            sent.append(lambda d=d: pl.when(came_from(source(d)))(hf(d).wait_send))
    for side, there in ((0, has_e), (1, has_w)):
        rows = dx_rows.at[pl.ds(0, WIDTH), mine]
        pl.when(there)(lambda side=side, rows=rows: arrived(rows, hf_r.at[side]))
    pl.when(has_e)(lambda: p_halo(0).wait_recv())
    pl.when(has_w)(lambda: p_halo(1).wait_recv())
    lax.fori_loop(0, WIDTH, begin, 0, unroll=True)
    lax.fori_loop(WIDTH + ROWS, TALL, begin, 0, unroll=True)

    lax.fori_loop(0, FIELDS, pack_rows(outside, True), 0, unroll=True)

    for step in range(1, STEPS + 1):
        def rows(j, carry, src=states[step - 1], dst=states[step], step=step):
            for b in (step + j, WIDTH + ROWS - step + j):
                stencil(src, dst, b, s0[b, METRIC], s0[b, MASK], level)
            return carry

        lax.fori_loop(0, WIDTH, rows, 0, unroll=True)

    for e, w in corners:
        pl.when(takes_corner[e, w])(lambda e=e, w=w: p_corner(e, w).wait_recv())
    for side, there in ((0, has_e), (1, has_w)):
        pl.when(there)(lambda side=side: arrived(cs.at[pl.ds(side * chips, chips)], cs_r.at[side]))
    by_core = [functools.reduce(jnp.add, [cs[2 * ch + co] for ch in range(chips)]) for co in range(2)]
    low = lane < COLS // 2
    from_south = jnp.where(low, by_core[0], by_core[1]) + (pcr[0, 0] + pcr[0, 1])
    from_north = pltpu.roll(jnp.where(low, by_core[1], by_core[0]), COLS // 2, 1) + (pcr[1, 0] + pcr[1, 1])
    for n, b in enumerate(outside):
        g, i = divmod(b, STRIP)
        left = jnp.logical_and(block == g, inner < WIDTH)
        right = jnp.logical_and(block == GROUPS + g, inner >= 16 - WIDTH)
        for f in range(FIELDS):
            at_lane = f * 32 + n * WIDTH
            strip = a0[i + 1, f]
            strip = jnp.where(left, pltpu.roll(from_south, (16 * g - at_lane) % COLS, 1), strip)
            strip = jnp.where(right, pltpu.roll(from_north, (76 + 16 * g - at_lane) % COLS, 1), strip)
            a0[i + 1, f] = strip
    for step in range(STEPS):
        src, dst = (a0, a1) if step % 2 == 0 else (a1, a0)
        for f in range(FIELDS):
            src[0, f] = pltpu.roll(src[STRIP, f], 16, 1)
            src[STRIP + 1, f] = pltpu.roll(src[1, f], COLS - 16, 1)

        def strip_row(i, carry, src=src, dst=dst):
            stencil(src, dst, i, a0[i, METRIC], a0[i, MASK], level)
            return carry

        lax.fori_loop(1, STRIP + 1, strip_row, 0, unroll=True)

    for g in range(GROUPS):
        def merge(i, carry, g=g):
            for f in range(FIELDS):
                strip = a0[i + 1, f]
                new = s4[g * STRIP + i, f]
                new = jnp.where(lane < WIDTH, pltpu.roll(strip, (-16 * g - WIDTH) % COLS, 1), new)
                new = jnp.where(lane >= COLS - WIDTH, pltpu.roll(strip, (52 - 16 * g) % COLS, 1), new)
                out[pl.ds(f * LEV * ROWS + g * STRIP + i - WIDTH, LEV, stride=ROWS), :] = new
            return carry

        lax.fori_loop(max(0, WIDTH - g * STRIP), min(STRIP, WIDTH + ROWS - g * STRIP), merge, 0, unroll=True)
    arrived(s0.at[pl.ds(0, pieces * part * HALF // (FIELDS + 2))], out_s)
    for wait in sent:
        wait()


def solution(mesh):
    members, nx, ny = (mesh.shape[axis] for axis in ("member", "dx", "dy"))
    chips = members // 2
    part = (ROWS // 2) // chips
    flat = FIELDS * LEV * ROWS

    def on_device(states, control, owner, map_factor, terrain):
        any_space = pl.BlockSpec(memory_space=pl.ANY)
        dma = pltpu.SemaphoreType.DMA
        out = pl.pallas_call(
            functools.partial(kernel, members, nx, ny),
            out_shape=pltpu.VMEM((flat, COLS), F32),
            in_specs=[any_space] * 5,
            out_specs=pl.BlockSpec(memory_space=pltpu.VMEM),
            scratch_shapes=[
                pltpu.VMEM((flat, COLS), F32),
                pltpu.VMEM((flat, COLS), F32),
                pltpu.SMEM((members,), jnp.int32),
                pltpu.VMEM((ROWS, COLS), F32),
                pltpu.VMEM((ROWS, COLS), jnp.int32),
                pltpu.VMEM((TALL, FIELDS + 2) + TILE, F32),
                pltpu.VMEM((TALL, FIELDS) + TILE, F32),
                pltpu.VMEM((TALL, FIELDS) + TILE, F32),
                pltpu.VMEM((TALL, FIELDS) + TILE, F32),
                pltpu.VMEM((TALL, FIELDS) + TILE, F32),
                pltpu.VMEM((ROWS, FIELDS) + TILE, F32),
                pltpu.VMEM((ROWS, HALF) + TILE, F32),
                pltpu.VMEM((ROWS, HALF) + TILE, F32),
                pltpu.VMEM((2, part * (chips - 1), HALF) + TILE, F32),
                pltpu.VMEM((TALL, FIELDS) + TILE, F32),
                pltpu.VMEM((2,) + TILE, F32),
                pltpu.VMEM((2,) + TILE, F32),
                pltpu.VMEM((STRIP + 2, FIELDS + 2) + TILE, F32),
                pltpu.VMEM((STRIP + 2, FIELDS) + TILE, F32),
                pltpu.VMEM((2, FIELDS + 2) + TILE, F32),
                pltpu.VMEM((2, FIELDS + 2) + TILE, F32),
                pltpu.VMEM((2, 2) + TILE, F32),
                pltpu.VMEM((2, 2) + TILE, F32),
                pltpu.VMEM((2,) + TILE, F32),
                pltpu.VMEM((2,) + TILE, F32),
                pltpu.VMEM(TILE, F32),
                pltpu.VMEM((members,) + TILE, F32),
                pltpu.VMEM((2 * WIDTH, FIELDS) + TILE, F32),
                dma((5,)),
                dma, dma((chips,)), dma, dma((2,)), dma((chips - 1,)), dma,
                dma, dma,
                dma, dma((chips - 1,)),
                dma((chips,)), dma((2,)),
                dma((2,)), dma((2,)),
                dma((2,)), dma((2,)),
                dma((4,)), dma((4,)),
                dma((2, 2)), dma((2, 2)),
                dma((2,)), dma((2,)),
                dma, dma((2,)),
                *[pltpu.SemaphoreType.REGULAR] * 4,
            ],
            compiler_params=pltpu.CompilerParams(collective_id=0, has_side_effects=True),
        )(states.reshape(flat, COLS), control.reshape(flat, COLS), owner, map_factor, terrain)
        return out.reshape(states.shape)

    spread = P("member", None, None, "dx", "dy")
    return jax.shard_map(
        on_device,
        mesh=mesh,
        in_specs=(spread, spread, P(), P("dx", "dy"), P("dx", "dy")),
        out_specs=spread,
        check_vma=False,
    )
```
